256 devices in a mesh: member: 16 (over z, y_lo), tile: 8 (over x, core), batch: 2 (over y_hi).
Axes of the slice: x: 4, y: 4 (y_hi: 2, y_lo: 2; y = y_hi * 2 + y_lo), z: 8, core: 2. Of those that a mesh axis runs over, the one named last changes fastest.
Arguments:
- latent: bfloat16 [16, 2, 8192, 1024], P('member', 'batch', 'tile'), may hold values from -6 to 6
- w_in: bfloat16 [1024, 1024], replicated, may hold values from -0.1875 to 0.1875
- w_out: bfloat16 [1024, 112], replicated, may hold values from -0.1875 to 0.1875
- observed: bfloat16 [2, 1024, 1792], P('batch', 'tile'), may hold values from -5 to 5
- patch_index: int32 [2, 512], P('batch', 'tile'), may hold values from 0 to 127
- counts: int32 [2, 512], P('batch', 'tile'), may hold values from 1 to 8
Outputs:
- grad_w1: float32 [1024, 1024], P(('member', 'tile', 'batch'))
- grad_w2: float32 [1024, 112], P(('member', 'tile', 'batch'))
The draws below stay inside these ranges and needn't reach their ends.
Inputs may be any that keep to these rules, and one draw needn't show every extreme that they name: `patch_index`: a candidate of the same tile and lead time.
All inputs are finite; a program needn't handle non-finite values.
Results may differ from the reference program's by a relative error of at most 0.0017.
Values sent between devices are 32-bit elements; how exact they have to be, the bound alone decides.
A program may use at most 64 MiB of HBM per device.

```python
import jax
import jax.numpy as jnp
from jax import lax

D = 1024
HID = 1024
CH = 112
PATCH = 16
POOL = 128
FEAT = 1792
SAMP = 64
MEMBERS = 16
LEADS = 2
CELLS = 8192
N_TILE = 8


def touch_ends(result, own_key, low, high):
    index_at = [jax.random.randint(jax.random.fold_in(own_key, axis), (), 0, length) for axis, length in enumerate(result.shape)]
    main_axis = result.shape.index(max(result.shape))
    beside = index_at[:main_axis] + [(index_at[main_axis] + 1) % result.shape[main_axis]] + index_at[main_axis + 1:]
    return result.at[tuple(index_at)].set(low).at[tuple(beside)].set(high)


def steps_of(own_key, extent, cuts, least, largest):
    def one(position, parts):
        heights = jax.random.uniform(jax.random.fold_in(jax.random.fold_in(own_key, 6), position), (parts,), jnp.float32, least / len(cuts), largest / len(cuts))
        return jnp.repeat(jnp.exp(heights), extent[position] // parts).reshape((-1,) + (1,) * (len(extent) - position - 1))

    level = one(*cuts[0])
    for cut in cuts[1:]:
        level = level * one(*cut)
    return level


def scatter_about(key, extent, spread, most, shards=(), kind=jnp.bfloat16):
    entries = jax.random.normal(key, extent, jnp.float32) * spread
    if len(shards) > 0:
        entries = steps_of(key, extent, shards, -0.22, 0.18) * entries
    return jnp.clip(entries, min=-most, max=most).astype(kind)


def setup_inputs(seed: int = 0) -> dict:
    splits = jax.random.split(jax.random.key(seed), 7)
    latent = scatter_about(splits[0], (MEMBERS, LEADS, CELLS, D), 1.0, 6.0, ((0, 16), (1, 2), (2, 8)))
    w_in = scatter_about(splits[1], (D, HID), D ** -0.5, 0.1875)
    w_out = scatter_about(splits[2], (HID, CH), HID ** -0.5, 0.1875)
    observed = scatter_about(splits[3], (LEADS, POOL * N_TILE, FEAT), 0.7, 5.0, ((0, 2), (1, 8)))
    patch_index = touch_ends(jax.random.randint(splits[4], (LEADS, SAMP * N_TILE), 0, POOL), jax.random.fold_in(splits[4], 1), 0, POOL - 1).astype(jnp.int32)
    counts = touch_ends(jax.random.randint(splits[5], (LEADS, SAMP * N_TILE), 1, 9), jax.random.fold_in(splits[5], 1), 1, 8).astype(jnp.int32)
    return {"latent": latent, "w_in": w_in, "w_out": w_out, "observed": observed, "patch_index": patch_index, "counts": counts}


def smooth_grad(deltas):
    return deltas / jnp.sqrt(lax.optimization_barrier(jnp.sum(deltas * deltas, axis=-1, keepdims=True)) + 1.0)

def decode(rows_in, w_in, w_out):
    preact = jnp.dot(rows_in, w_in, preferred_element_type=jnp.float32)
    hidden = jax.nn.silu(preact).astype(jnp.bfloat16)
    decoded = jnp.dot(hidden, w_out, preferred_element_type=jnp.float32)
    return (preact, hidden, decoded)

def reference(latent, w_in, w_out, observed, patch_index, counts):
    npatch = CELLS // PATCH
    flat_latent = latent.reshape(MEMBERS, LEADS * CELLS, D)

    def forward(rows_in):
        return decode(rows_in, w_in, w_out)[2]
    decoded = lax.map(forward, flat_latent)
    patches = decoded.reshape(MEMBERS, LEADS, npatch, PATCH * CH)
    tiles = jnp.arange(npatch, dtype=jnp.int32) // SAMP * POOL
    picked = (patch_index + tiles[None, :]).astype(jnp.int32)
    target = jnp.take_along_axis(observed, picked[:, :, None], axis=1).astype(jnp.float32)
    own = smooth_grad(patches - target[None])

    def pair_of(single):
        return lax.optimization_barrier(jnp.sum(smooth_grad(single[None] - patches), axis=0))
    pair = lax.map(pair_of, patches)
    weight = counts.astype(jnp.float32)[None, :, :, None]
    grad_patch = weight * (own / MEMBERS - pair / (MEMBERS * MEMBERS))
    grad_decoded = grad_patch.reshape(MEMBERS, LEADS * CELLS, CH).astype(jnp.bfloat16)

    def accumulate(totals, inputs):
        rows_in, grad_out = inputs
        preact, hidden, decoded_rows = decode(rows_in, w_in, w_out)
        grad_hidden = lax.dot_general(grad_out, w_out, (((1,), (1,)), ((), ())), preferred_element_type=jnp.float32)
        sigma = jax.nn.sigmoid(preact)
        grad_preact = (grad_hidden * sigma * (1.0 + preact * (1.0 - sigma))).astype(jnp.bfloat16)
        first = lax.dot_general(rows_in, grad_preact, (((0,), (0,)), ((), ())), preferred_element_type=jnp.float32)
        second = lax.dot_general(hidden, grad_out, (((0,), (0,)), ((), ())), preferred_element_type=jnp.float32)
        return ((totals[0] + first, totals[1] + second), None)
    start = (jnp.zeros((D, HID), jnp.float32), jnp.zeros((HID, CH), jnp.float32))
    totals, unused = lax.scan(accumulate, start, (flat_latent, grad_decoded))
    return (totals[0], totals[1])
```

```python
import jax
import jax.numpy as jnp
from jax import lax
from jax.experimental import pallas as pl
from jax.experimental.pallas import tpu as pltpu
from jax.sharding import PartitionSpec as P

MESH = pl.DeviceIdType.MESH
F32, BF16 = jnp.float32, jnp.bfloat16
ROWS, D, HID, CH, LANE = 1024, 1024, 1024, 112, 128
PATCH, NPATCH, MEMBERS, POOL, FEAT = 16, 64, 16, 128, 1792
NCHUNK, CROWS = 4, 256
ORDER = (1, 15, 2, 14, 3, 13, 4, 12, 5, 11, 6, 10, 7, 9, 8)
PAIRS = [(i, k) for i in range(MEMBERS) for k in range(i + 1, MEMBERS)]
PAIR_AT = {pair: at for at, pair in enumerate(PAIRS)}


def forward_chunk(c, lat, w_in, wo, pre, hid, dec):
    rows = pl.ds(pl.multiple_of(c * CROWS, CROWS), CROWS)
    for n in range(4):
        cols = slice(n * 256, n * 256 + 256)
        v = jnp.dot(lat[rows, :], w_in[:, cols], preferred_element_type=F32)
        pre[rows, cols] = v
        hid[rows, cols] = (v * (1.0 / (1.0 + jnp.exp(-v)))).astype(BF16)
    out = jnp.dot(hid[rows, :], wo[...], preferred_element_type=F32)
    dec[c] = out.reshape(MEMBERS, PATCH, LANE)


def slopes(pre):
    def step(i, carry):
        rows = pl.ds(pl.multiple_of(i * 64, 64), 64)
        v = pre[rows, :]
        sigma = 1.0 / (1.0 + jnp.exp(-v))
        pre[rows, :] = sigma * (1.0 + v * (1.0 - sigma))
        return carry

    lax.fori_loop(0, ROWS // 64, step, 0)


def transposed(src, dst):
    def step(i, carry):
        at = pl.ds(pl.multiple_of(i * 128, 128), 128)
        dst[at, :] = src[:, at].T
        return carry

    lax.fori_loop(0, 8, step, 0)


def own_term(obs, idx, cnt, dec, tgt, target, own, weight):
    pool_at = lax.broadcasted_iota(jnp.int32, (POOL, NPATCH), 0)
    choose = (pool_at == idx[...]).astype(F32).astype(BF16)
    picked = lax.dot_general(choose, obs[...], (((0,), (0,)), ((), ())), preferred_element_type=F32)
    tgt[...] = picked.astype(BF16)
    entry = lax.broadcasted_iota(jnp.int32, (256, LANE), 0)
    lane = lax.broadcasted_iota(jnp.int32, (256, LANE), 1)
    for i in range(PATCH):
        start = min(CH * i // 128 * 128, FEAT - 256)
        shift = ((entry == lane + (CH * i - start)) & (lane < CH)).astype(F32).astype(BF16)
        one = jnp.dot(tgt[:, start : start + 256], shift, preferred_element_type=F32)
        target[pl.ds(i, NPATCH, stride=PATCH), :] = one
    counts = cnt[...].astype(F32)

    def step(c, carry):
        rows = pl.ds(pl.multiple_of(c * CROWS, CROWS), CROWS)
        patch_of = (lax.broadcasted_iota(jnp.int32, (CROWS, NPATCH), 0) + c * CROWS) // PATCH
        at = lax.broadcasted_iota(jnp.int32, (CROWS, NPATCH), 1)
        count = jnp.sum(jnp.where(patch_of == at, counts, 0.0), axis=1, keepdims=True)
        delta = dec[c].reshape(CROWS, LANE) - target[rows, :]
        square = jnp.sum((delta * delta).reshape(MEMBERS, PATCH, LANE), axis=(1, 2), keepdims=True)
        scale = (1.0 / (MEMBERS * jnp.sqrt(square + 1.0))) * jnp.ones((MEMBERS, PATCH, LANE), F32)
        own[rows, :] = delta * scale.reshape(CROWS, LANE) * count
        weight[rows, :] = jnp.broadcast_to(count * (1.0 / (MEMBERS * MEMBERS)), (CROWS, LANE))
        return carry

    lax.fori_loop(0, NCHUNK, step, 0)


def pair_patch(c, x, part, inv, out):
    xs = [x[k, c] for k in range(MEMBERS)]
    for at, (i, k) in enumerate(PAIRS):
        d = xs[i] - xs[k]
        d = d * d
        part[at] = d[:8] + d[8:]
    total = jnp.sum(jnp.sum(part[...], axis=1), axis=1, keepdims=True)
    inv[...] = jnp.broadcast_to(1.0 / jnp.sqrt(total + 1.0), inv.shape)
    for i in range(MEMBERS):
        acc = None
        for k in range(MEMBERS):
            if k == i:
                continue
            at = PAIR_AT[(min(i, k), max(i, k))]
            term = (xs[i] - xs[k]) * inv[at : at + 1, :]
            acc = term if acc is None else acc + term
        out[c, i] = acc


def backward_chunk(c, back, own, weight, wo_t, slope, go, gp):
    rows = pl.ds(pl.multiple_of(c * CROWS, CROWS), CROWS)
    pair = back[c].reshape(CROWS, LANE)
    grad = (own[rows, :] - weight[rows, :] * pair).astype(BF16)
    go[rows, :] = grad
    for n in range(4):
        cols = slice(n * 256, n * 256 + 256)
        gh = jnp.dot(grad, wo_t[:, cols], preferred_element_type=F32)
        gp[rows, cols] = (gh * slope[rows, cols]).astype(BF16)


def halves(lo, hi):
    top = lax.broadcasted_iota(jnp.int32, lo.shape, lo.ndim - 2) < 4
    axis = lo.ndim - 2
    return jnp.where(top, lo, pltpu.roll(hi, 4, axis)), jnp.where(top, pltpu.roll(lo, 4, axis), hi)


def weight_grad(left, right, cols, half, put):
    def step(z, carry):
        at = pl.ds(pl.multiple_of(z * 128, 128), 128)
        g = jnp.dot(left[at, :], right[:, cols], preferred_element_type=F32)
        g = g.reshape(16, 8, g.shape[1])
        if half == 0:
            first, second = g, pltpu.roll(g, 4, 1)
        else:
            first, second = halves(g[:, :, :half], g[:, :, half:])
        for lo in range(2):
            for x in range(4):
                for core in range(2):
                    put(core, x, lo, z, first[(lo * 4 + x) * 2 + core])
                    put(core, x, 2 + lo, z, second[(lo * 4 + x) * 2 + core])
        return carry

    lax.fori_loop(0, 8, step, 0)


def kernel(
    lat_hbm, w_in_hbm, w_out_hbm, obs_hbm, idx_hbm, cnt_hbm, out1, out2,
    lat, w_in, w_raw, wo, wo_t, obs, idx, cnt, pre, hid, dec, x, tgt, target, own, weight, part, inv, ret, back,
    go, gp, lat_t, hid_t, qa, qb, qc, a0, b0, c0, a1, b1, c1, a2, b2, c2, a3, b3, c3,
    load_sem, there_send, there_recv, back_send, back_recv, rs_send, rs_recv,
):
    m, t, b = lax.axis_index("member"), lax.axis_index("tile"), lax.axis_index("batch")
    z, y_lo, xx, core = m // 2, m % 2, t // 2, t % 2
    y = b * 2 + y_lo

    def at_x(o):
        return {"tile": (xx + o) % 4 * 2 + core}

    def at_y(o):
        to = (y + o) % 4
        return {"member": z * 2 + to % 2, "batch": to // 2}

    def at_z(o):
        return {"member": (z + o) % 8 * 2 + y_lo}

    def at_member(o):
        return {"member": (m + o) % MEMBERS}

    def at_core():
        return {"tile": xx * 2 + (1 - core)}

    barrier = pltpu.get_barrier_semaphore()
    peers = [at_member(o) for o in range(1, 16)] + [at_core()] + [at_x(o) for o in range(1, 4)]
    for peer in peers:
        pl.semaphore_signal(barrier, inc=1, device_id=peer, device_id_type=MESH)
    for o in (1, 2, 3):
        pl.semaphore_signal(barrier, inc=1, device_id=at_y(o), device_id_type=MESH)

    loads = [pltpu.make_async_copy(w_in_hbm, w_in, load_sem.at[0])]
    for c in range(NCHUNK):
        rows = pl.ds(c * CROWS, CROWS)
        loads.append(pltpu.make_async_copy(lat_hbm.at[0, 0, rows, :], lat.at[rows, :], load_sem.at[1 + c]))
    loads.append(pltpu.make_async_copy(w_out_hbm, w_raw, load_sem.at[5]))
    loads.append(pltpu.make_async_copy(obs_hbm.at[0], obs, load_sem.at[6]))
    loads.append(pltpu.make_async_copy(idx_hbm, idx, load_sem.at[7]))
    loads.append(pltpu.make_async_copy(cnt_hbm, cnt, load_sem.at[8]))
    for load in loads:
        load.start()
    wo[...] = jnp.zeros(wo.shape, wo.dtype)
    loads[5].wait()
    wo[:, :CH] = w_raw[...]
    for load in loads[:5]:
        load.wait()
    pl.semaphore_wait(barrier, len(peers) + 3)

    def there(c, o):
        return pltpu.make_async_remote_copy(
            src_ref=dec.at[c, (m + o) % MEMBERS], dst_ref=x.at[m, c],
            send_sem=there_send.at[c, o], recv_sem=there_recv.at[c, o],
            device_id=at_member(o), device_id_type=MESH,
        )

    def returned(c, o):
        return pltpu.make_async_remote_copy(
            src_ref=ret.at[c, (m + o) % MEMBERS], dst_ref=back.at[c, m],
            send_sem=back_send.at[c, o], recv_sem=back_recv.at[c, o],
            device_id=at_member(o), device_id_type=MESH,
        )

    def forward(c, carry):
        forward_chunk(c, lat, w_in, wo, pre, hid, dec)
        x[m, c] = dec[c, m]
        for o in ORDER:
            there(c, o).start()
        return carry

    lax.fori_loop(0, NCHUNK, forward, 0)

    for load in loads[6:]:
        load.wait()
    wo_t[...] = wo[...].T
    own_term(obs, idx, cnt, dec, tgt, target, own, weight)
    slopes(pre)
    transposed(hid, hid_t)
    transposed(lat, lat_t)

    def arrived(make):
        def step(c, carry):
            for o in range(1, MEMBERS):
                make(c, o).wait_recv()
            return carry

        return step

    lax.fori_loop(0, NCHUNK, arrived(there), 0)

    def score(c, carry):
        pair_patch(c, x, part, inv, ret)
        back[c, m] = ret[c, m]
        for o in ORDER:
            returned(c, o).start()
        return carry

    lax.fori_loop(0, NCHUNK, score, 0)

    def backward(c, carry):
        arrived(returned)(c, 0)
        backward_chunk(c, back, own, weight, wo_t, pre, go, gp)
        return carry

    lax.fori_loop(0, NCHUNK, backward, 0)

    slots = iter(range(45))

    def send(src, dst, device):
        at = next(slots)
        copy = pltpu.make_async_remote_copy(
            src_ref=src, dst_ref=dst, send_sem=rs_send.at[at], recv_sem=rs_recv.at[at],
            device_id=device, device_id_type=MESH,
        )
        copy.start()
        sent.append(copy)
        return copy

    sent = []

    def added(own_ref, landed, copies):
        for copy in copies:
            copy.wait_recv()
        n = own_ref.shape[0]

        def step(i, carry):
            total = own_ref[i]
            for j in range(landed.shape[0]):
                total = total + landed[j, i]
            own_ref[i] = total
            return carry

        lax.fori_loop(0, n, step, 0)

    def put_a(k, x_, y_, z_, value):
        qa[k, x_, y_, z_] = value

    def put_b(k, x_, y_, z_, value):
        qb[k, y_, x_, z_] = value

    def put_c(k, x_, y_, z_, value):
        qc[k, z_, x_, y_] = value

    weight_grad(hid_t, go, slice(0, 128), 0, put_c)
    c_core = send(qc.at[1 - core], c0.at[0], at_core())
    weight_grad(lat_t, gp, slice(0, 512), 256, put_a)
    a_core = send(qa.at[1 - core], a0.at[0], at_core())
    added(qc.at[core], c0, [c_core])
    c_one = [send(qc.at[core, (z + o) % 8], c1.at[o - 1], at_z(o)) for o in (4, 3, 5, 2, 6, 1, 7)]
    weight_grad(lat_t, gp, slice(512, 1024), 256, put_b)
    b_core = send(qb.at[1 - core], b0.at[0], at_core())
    added(qa.at[core], a0, [a_core])
    a_one = [send(qa.at[core, (xx + o) % 4], a1.at[o - 1], at_x(o)) for o in (2, 1, 3)]
    added(qb.at[core], b0, [b_core])
    b_one = [send(qb.at[core, (y + o) % 4], b1.at[o - 1], at_y(o)) for o in (2, 1, 3)]
    added(qc.at[core, z], c1, c_one)
    c_two = [send(qc.at[core, z, (xx + o) % 4], c2.at[o - 1], at_x(o)) for o in (2, 1, 3)]
    added(qa.at[core, xx], a1, a_one)
    a_two = [send(qa.at[core, xx, (y + o) % 4], a2.at[o - 1], at_y(o)) for o in (2, 1, 3)]
    added(qb.at[core, y], b1, b_one)
    b_two = [send(qb.at[core, y, (xx + o) % 4], b2.at[o - 1], at_x(o)) for o in (2, 1, 3)]
    added(qc.at[core, z, xx], c2, c_two)
    c_three = [send(qc.at[core, z, xx, (y + o) % 4], c3.at[o - 1], at_y(o)) for o in (2, 1, 3)]
    added(qa.at[core, xx, y], a2, a_two)
    a_three = [send(qa.at[core, xx, y, (z + o) % 8], a3.at[o - 1], at_z(o)) for o in (4, 3, 5, 2, 6, 1, 7)]
    added(qb.at[core, y, xx], b2, b_two)
    b_three = [send(qb.at[core, y, xx, (z + o) % 8], b3.at[o - 1], at_z(o)) for o in (4, 3, 5, 2, 6, 1, 7)]

    def last(value, landed, copies):
        for copy in copies:
            copy.wait_recv()
        for j in range(landed.shape[0]):
            value = value + landed[j]
        return value

    total = last(qc[core, z, xx, y], c3, c_three)
    out2[...] = total[:4, :CH]
    total = last(qa[core, xx, y, z], a3, a_three)
    out1[:, 0:256] = total[:4]
    out1[:, 256:512] = pltpu.roll(total, 4, 0)[:4]
    total = last(qb[core, y, xx, z], b3, b_three)
    out1[:, 512:768] = total[:4]
    out1[:, 768:1024] = pltpu.roll(total, 4, 0)[:4]

    for copy in sent:
        copy.wait_send()

    def drained(c, carry):
        for o in range(1, MEMBERS):
            there(c, o).wait_send()
            returned(c, o).wait_send()
        return carry

    lax.fori_loop(0, NCHUNK, drained, 0)


def scratch():
    v = pltpu.VMEM
    return [
        v((ROWS, D), BF16), v((D, HID), BF16), v((HID, CH), BF16), v((HID, LANE), BF16), v((LANE, HID), BF16),
        v((POOL, FEAT), BF16), v((1, NPATCH), jnp.int32), v((1, NPATCH), jnp.int32),
        v((ROWS, HID), F32), v((ROWS, HID), BF16), v((NCHUNK, MEMBERS, PATCH, LANE), F32),
        v((MEMBERS, NCHUNK, PATCH, LANE), F32), v((NPATCH, FEAT), BF16), v((ROWS, LANE), F32),
        v((ROWS, LANE), F32), v((ROWS, LANE), F32), v((len(PAIRS), 8, LANE), F32), v((len(PAIRS), LANE), F32),
        v((NCHUNK, MEMBERS, PATCH, LANE), F32), v((NCHUNK, MEMBERS, PATCH, LANE), F32),
        v((ROWS, LANE), BF16), v((ROWS, HID), BF16), v((D, ROWS), BF16), v((HID, ROWS), BF16),
        v((2, 4, 4, 8, 8, 256), F32), v((2, 4, 4, 8, 8, 256), F32), v((2, 8, 4, 4, 8, 128), F32),
        v((1, 4, 4, 8, 8, 256), F32), v((1, 4, 4, 8, 8, 256), F32), v((1, 8, 4, 4, 8, 128), F32),
        v((3, 4, 8, 8, 256), F32), v((3, 4, 8, 8, 256), F32), v((7, 4, 4, 8, 128), F32),
        v((3, 8, 8, 256), F32), v((3, 8, 8, 256), F32), v((3, 4, 8, 128), F32),
        v((7, 8, 256), F32), v((7, 8, 256), F32), v((3, 8, 128), F32),
        pltpu.SemaphoreType.DMA((9,)),
        pltpu.SemaphoreType.DMA((NCHUNK, MEMBERS)), pltpu.SemaphoreType.DMA((NCHUNK, MEMBERS)),
        pltpu.SemaphoreType.DMA((NCHUNK, MEMBERS)), pltpu.SemaphoreType.DMA((NCHUNK, MEMBERS)),
        pltpu.SemaphoreType.DMA((45,)), pltpu.SemaphoreType.DMA((45,)),
    ]


def shards(latent, w_in, w_out, observed, patch_index, counts):
    return pl.pallas_call(
        kernel,
        out_shape=(jax.ShapeDtypeStruct((4, HID), F32), jax.ShapeDtypeStruct((4, CH), F32)),
        in_specs=[pl.BlockSpec(memory_space=pl.ANY)] * 6,
        out_specs=(pl.BlockSpec(memory_space=pltpu.VMEM), pl.BlockSpec(memory_space=pltpu.VMEM)),
        scratch_shapes=scratch(),
        compiler_params=pltpu.CompilerParams(
            collective_id=0, has_side_effects=True, vmem_limit_bytes=60 * 1024 * 1024
        ),
    )(latent, w_in, w_out, observed, patch_index, counts)


def solution(mesh):
    placed = (
        P("member", "batch", "tile", None),
        P(),
        P(),
        P("batch", "tile", None),
        P("batch", "tile"),
        P("batch", "tile"),
    )
    rows = P(("member", "tile", "batch"), None)
    return jax.shard_map(
        shards, mesh=mesh, in_specs=placed, out_specs=(rows, rows), check_vma=False
    )
```

```python
import jax
import jax.numpy as jnp
from jax import lax
from jax.experimental import pallas as pl
from jax.experimental.pallas import tpu as pltpu
from jax.sharding import PartitionSpec as P

MESH = pl.DeviceIdType.MESH
F32, BF16 = jnp.float32, jnp.bfloat16
ROWS, D, HID, CH, LANE = 1024, 1024, 1024, 112, 128
PATCH, NPATCH, MEMBERS, POOL, FEAT = 16, 64, 16, 128, 1792
NCHUNK, CROWS = 4, 256
ORDER = (1, 15, 2, 14, 3, 13, 4, 12, 5, 11, 6, 10, 7, 9, 8)
PAIRS = [(i, k) for i in range(MEMBERS) for k in range(i + 1, MEMBERS)]
PAIR_AT = {pair: at for at, pair in enumerate(PAIRS)}


def forward_chunk(c, lat, w_in, wo, pre, hid, dec):
    rows = pl.ds(pl.multiple_of(c * CROWS, CROWS), CROWS)
    v = jnp.dot(lat[rows, :], w_in[...], preferred_element_type=F32)
    pre[rows, :] = v
    hid[rows, :] = (v * (1.0 / (1.0 + jnp.exp(-v)))).astype(BF16)
    out = jnp.dot(hid[rows, :], wo[...], preferred_element_type=F32)
    dec[c] = out.reshape(MEMBERS, PATCH, LANE)


def slopes(pre):
    def step(i, carry):
        rows = pl.ds(pl.multiple_of(i * 64, 64), 64)
        v = pre[rows, :]
        sigma = 1.0 / (1.0 + jnp.exp(-v))
        pre[rows, :] = sigma * (1.0 + v * (1.0 - sigma))
        return carry

    lax.fori_loop(0, ROWS // 64, step, 0)


def transposed(src, dst):
    def step(i, carry):
        at = pl.ds(pl.multiple_of(i * 128, 128), 128)
        dst[at, :] = src[:, at].T
        return carry

    lax.fori_loop(0, 8, step, 0)


def own_term(obs, idx, cnt, dec, tgt, target, own, weight):
    pool_at = lax.broadcasted_iota(jnp.int32, (POOL, NPATCH), 0)
    choose = (pool_at == idx[...]).astype(F32).astype(BF16)
    picked = lax.dot_general(choose, obs[...], (((0,), (0,)), ((), ())), preferred_element_type=F32)
    tgt[...] = picked.astype(BF16)
    entry = lax.broadcasted_iota(jnp.int32, (256, LANE), 0)
    lane = lax.broadcasted_iota(jnp.int32, (256, LANE), 1)
    for i in range(PATCH):
        start = min(CH * i // 128 * 128, FEAT - 256)
        shift = ((entry == lane + (CH * i - start)) & (lane < CH)).astype(F32).astype(BF16)
        one = jnp.dot(tgt[:, start : start + 256], shift, preferred_element_type=F32)
        target[pl.ds(i, NPATCH, stride=PATCH), :] = one
    counts = cnt[...].astype(F32)

    def step(c, carry):
        rows = pl.ds(pl.multiple_of(c * CROWS, CROWS), CROWS)
        patch_of = (lax.broadcasted_iota(jnp.int32, (CROWS, NPATCH), 0) + c * CROWS) // PATCH
        at = lax.broadcasted_iota(jnp.int32, (CROWS, NPATCH), 1)
        count = jnp.sum(jnp.where(patch_of == at, counts, 0.0), axis=1, keepdims=True)
        delta = dec[c].reshape(CROWS, LANE) - target[rows, :]
        square = jnp.sum((delta * delta).reshape(MEMBERS, PATCH, LANE), axis=(1, 2), keepdims=True)
        scale = (1.0 / (MEMBERS * jnp.sqrt(square + 1.0))) * jnp.ones((MEMBERS, PATCH, LANE), F32)
        own[rows, :] = delta * scale.reshape(CROWS, LANE) * count
        weight[rows, :] = jnp.broadcast_to(count * (1.0 / (MEMBERS * MEMBERS)), (CROWS, LANE))
        return carry

    lax.fori_loop(0, NCHUNK, step, 0)


def pair_patch(c, x, part, inv, out):
    xs = [x[k, c] for k in range(MEMBERS)]
    for at, (i, k) in enumerate(PAIRS):
        d = xs[i] - xs[k]
        d = d * d
        part[at] = d[:8] + d[8:]
    total = jnp.sum(jnp.sum(part[...], axis=1), axis=1, keepdims=True)
    inv[...] = jnp.broadcast_to(1.0 / jnp.sqrt(total + 1.0), inv.shape)
    for i in range(MEMBERS):
        acc = None
        for k in range(MEMBERS):
            if k == i:
                continue
            at = PAIR_AT[(min(i, k), max(i, k))]
            term = (xs[i] - xs[k]) * inv[at : at + 1, :]
            acc = term if acc is None else acc + term
        out[c, i] = acc


def backward_chunk(c, back, own, weight, wo_t, slope, go, gp):
    rows = pl.ds(pl.multiple_of(c * CROWS, CROWS), CROWS)
    pair = back[c].reshape(CROWS, LANE)
    grad = (own[rows, :] - weight[rows, :] * pair).astype(BF16)
    go[rows, :] = grad
    gh = jnp.dot(grad, wo_t[...], preferred_element_type=F32)
    gp[rows, :] = (gh * slope[rows, :]).astype(BF16)


def accumulate(c, left, right, total):
    rows = pl.ds(pl.multiple_of(c * CROWS, CROWS), CROWS)

    def step(i, carry):
        at = pl.ds(pl.multiple_of(i * 256, 256), 256)
        total[at, :] += jnp.dot(left[at, rows], right[rows, :], preferred_element_type=F32)
        return carry

    lax.fori_loop(0, 4, step, 0)


def halves(lo, hi):
    top = lax.broadcasted_iota(jnp.int32, lo.shape, lo.ndim - 2) < 4
    axis = lo.ndim - 2
    return jnp.where(top, lo, pltpu.roll(hi, 4, axis)), jnp.where(top, pltpu.roll(lo, 4, axis), hi)


def last_chunk(left, right, total, cols, put):
    rows = slice((NCHUNK - 1) * CROWS, NCHUNK * CROWS)

    def step(i, carry):
        at = pl.ds(pl.multiple_of(i * 256, 256), 256)
        g = total[at, cols] + jnp.dot(left[at, rows], right[rows, cols], preferred_element_type=F32)
        g = g.reshape(2, 2, 4, 2, 8, g.shape[1])
        for j in range(2):
            put(i * 2 + j, g[j])
        return carry

    lax.fori_loop(0, 4, step, 0)


def kernel(
    lat_hbm, w_in_hbm, w_out_hbm, obs_hbm, idx_hbm, cnt_hbm, out,
    lat, w_in, w_raw, wo, wo_t, obs, idx, cnt, pre, hid, dec, x, tgt, target, own, weight, part, inv, ret, back,
    go, gp, lat_t, hid_t, sum1, sum2, qa, qb, qc, a0, b0, c0, a1, b1, c1, a2, b2, c2, a3, b3, c3,
    load_sem, there_send, there_recv, back_send, back_recv, rs_send, rs_recv,
):
    m, t, b = lax.axis_index("member"), lax.axis_index("tile"), lax.axis_index("batch")
    z, y_lo, xx, core = m // 2, m % 2, t // 2, t % 2
    y = b * 2 + y_lo

    def at_x(o):
        return {"tile": (xx + o) % 4 * 2 + core}

    def at_y(o):
        to = (y + o) % 4
        return {"member": z * 2 + to % 2, "batch": to // 2}

    def at_z(o):
        return {"member": (z + o) % 8 * 2 + y_lo}

    def at_member(o):
        return {"member": (m + o) % MEMBERS}

    def at_core():
        return {"tile": xx * 2 + (1 - core)}

    barrier = pltpu.get_barrier_semaphore()
    peers = [at_member(o) for o in range(1, 16)] + [at_core()] + [at_x(o) for o in range(1, 4)]
    for peer in peers:
        pl.semaphore_signal(barrier, inc=1, device_id=peer, device_id_type=MESH)
    for o in (1, 2, 3):
        pl.semaphore_signal(barrier, inc=1, device_id=at_y(o), device_id_type=MESH)

    def load_lat(c):
        rows = pl.ds(pl.multiple_of(c * CROWS, CROWS), CROWS)
        return pltpu.make_async_copy(lat_hbm.at[0, 0, rows, :], lat.at[rows, :], load_sem.at[c])

    load_w = pltpu.make_async_copy(w_in_hbm, w_in, load_sem.at[4])
    load_wo = pltpu.make_async_copy(w_out_hbm, w_raw, load_sem.at[5])
    later = [
        pltpu.make_async_copy(obs_hbm.at[0], obs, load_sem.at[6]),
        pltpu.make_async_copy(idx_hbm, idx, load_sem.at[7]),
        pltpu.make_async_copy(cnt_hbm, cnt, load_sem.at[8]),
    ]
    load_wo.start()
    load_w.start()
    for c in range(NCHUNK):
        load_lat(c).start()
    for load in later:
        load.start()
    wo_t[CH:, :] = jnp.zeros((LANE - CH, HID), BF16)
    load_wo.wait()
    wo_t[:CH, :] = w_raw[...]
    wo[...] = wo_t[...].T
    load_w.wait()

    def there(c, o):
        return pltpu.make_async_remote_copy(
            src_ref=dec.at[c, (m + o) % MEMBERS], dst_ref=x.at[m, c],
            send_sem=there_send.at[c, o], recv_sem=there_recv.at[c, o],
            device_id=at_member(o), device_id_type=MESH,
        )

    def returned(c, o):
        return pltpu.make_async_remote_copy(
            src_ref=ret.at[c, (m + o) % MEMBERS], dst_ref=back.at[c, m],
            send_sem=back_send.at[c, o], recv_sem=back_recv.at[c, o],
            device_id=at_member(o), device_id_type=MESH,
        )

    def arrived(make, c):
        for o in range(1, MEMBERS):
            make(c, o).wait_recv()

    def forward(c, carry):
        load_lat(c).wait()
        forward_chunk(c, lat, w_in, wo, pre, hid, dec)
        return carry

    def depart(c):
        x[m, c] = dec[c, m]
        for o in ORDER:
            there(c, o).start()

    def forward_and_depart(c, carry):
        forward(c, carry)
        depart(c)
        return carry

    forward(0, 0)
    pl.semaphore_wait(barrier, len(peers) + 3)
    depart(0)
    lax.fori_loop(1, NCHUNK, forward_and_depart, 0)

    for load in later:
        load.wait()
    own_term(obs, idx, cnt, dec, tgt, target, own, weight)
    slopes(pre)
    transposed(hid, hid_t)
    transposed(lat, lat_t)
    sum1[...] = jnp.zeros(sum1.shape, F32)
    sum2[...] = jnp.zeros(sum2.shape, F32)

    def score(c, carry):
        arrived(there, c)
        pair_patch(c, x, part, inv, ret)
        back[c, m] = ret[c, m]
        for o in ORDER:
            returned(c, o).start()
        return carry

    lax.fori_loop(0, NCHUNK, score, 0)

    def backward(c, carry):
        arrived(returned, c)
        backward_chunk(c, back, own, weight, wo_t, pre, go, gp)
        accumulate(c, hid_t, go, sum2)
        accumulate(c, lat_t, gp, sum1)
        return carry

    lax.fori_loop(0, NCHUNK - 1, backward, 0)
    arrived(returned, NCHUNK - 1)
    backward_chunk(NCHUNK - 1, back, own, weight, wo_t, pre, go, gp)

    slots = iter(range(45))

    def send(src, dst, device):
        at = next(slots)
        copy = pltpu.make_async_remote_copy(
            src_ref=src, dst_ref=dst, send_sem=rs_send.at[at], recv_sem=rs_recv.at[at],
            device_id=device, device_id_type=MESH,
        )
        copy.start()
        sent.append(copy)
        return copy

    sent = []

    def added(own_ref, landed, copies):
        for copy in copies:
            copy.wait_recv()
        n = own_ref.shape[0]

        def step(i, carry):
            total = own_ref[i]
            for j in range(landed.shape[0]):
                total = total + landed[j, i]
            own_ref[i] = total
            return carry

        lax.fori_loop(0, n, step, 0)

    def put_a(k, g):
        first, second = halves(g[..., :256], g[..., 256:])
        for lo in range(2):
            for x_ in range(4):
                for core_ in range(2):
                    qa[core_, x_, lo, k] = first[lo, x_, core_]
                    qa[core_, x_, 2 + lo, k] = second[lo, x_, core_]

    def put_b(k, g):
        first, second = halves(g[..., :256], g[..., 256:])
        for lo in range(2):
            for x_ in range(4):
                for core_ in range(2):
                    qb[core_, lo, x_, k] = first[lo, x_, core_]
                    qb[core_, 2 + lo, x_, k] = second[lo, x_, core_]

    def put_c(k, g):
        first, second = halves(g[0], g[1])
        for x_ in range(4):
            for core_ in range(2):
                qc[core_, k, x_, 0] = first[x_, core_]
                qc[core_, k, x_, 1] = second[x_, core_]

    last_chunk(hid_t, go, sum2, slice(0, LANE), put_c)
    c_core = send(qc.at[1 - core], c0.at[0], at_core())
    last_chunk(lat_t, gp, sum1, slice(0, 512), put_a)
    a_core = send(qa.at[1 - core], a0.at[0], at_core())
    added(qc.at[core], c0, [c_core])
    c_one = [send(qc.at[core, (z + o) % 8], c1.at[o - 1], at_z(o)) for o in (4, 3, 5, 2, 6, 1, 7)]
    last_chunk(lat_t, gp, sum1, slice(512, 1024), put_b)
    b_core = send(qb.at[1 - core], b0.at[0], at_core())
    added(qa.at[core], a0, [a_core])
    a_one = [send(qa.at[core, (xx + o) % 4], a1.at[o - 1], at_x(o)) for o in (2, 1, 3)]
    added(qb.at[core], b0, [b_core])
    b_one = [send(qb.at[core, (y + o) % 4], b1.at[o - 1], at_y(o)) for o in (2, 1, 3)]
    added(qc.at[core, z], c1, c_one)
    c_two = [send(qc.at[core, z, (xx + o) % 4], c2.at[o - 1], at_x(o)) for o in (2, 1, 3)]
    added(qa.at[core, xx], a1, a_one)
    a_two = [send(qa.at[core, xx, (y + o) % 4], a2.at[o - 1], at_y(o)) for o in (2, 1, 3)]
    added(qb.at[core, y], b1, b_one)
    b_two = [send(qb.at[core, y, (xx + o) % 4], b2.at[o - 1], at_x(o)) for o in (2, 1, 3)]
    added(qc.at[core, z, xx], c2, c_two)
    c_three = [send(qc.at[core, z, xx, (y + o) % 4 // 2], c3.at[o - 1], at_y(o)) for o in (2, 1, 3)]
    added(qa.at[core, xx, y], a2, a_two)
    a_three = [send(qa.at[core, xx, y, (z + o) % 8], a3.at[o - 1], at_z(o)) for o in (4, 3, 5, 2, 6, 1, 7)]
    added(qb.at[core, y, xx], b2, b_two)
    b_three = [send(qb.at[core, y, xx, (z + o) % 8], b3.at[o - 1], at_z(o)) for o in (4, 3, 5, 2, 6, 1, 7)]

    def last(value, landed, copies):
        for copy in copies:
            copy.wait_recv()
        for j in range(landed.shape[0]):
            value = value + landed[j]
        return value

    total = last(qc[core, z, xx, b], c3, c_three)
    out[:, 512:] = jnp.where(y_lo == 0, total, pltpu.roll(total, 4, 0))
    out[:, :256] = last(qa[core, xx, y, z], a3, a_three)
    out[:, 256:512] = last(qb[core, y, xx, z], b3, b_three)

    for copy in sent:
        copy.wait_send()

    def drained(c, carry):
        for o in range(1, MEMBERS):
            there(c, o).wait_send()
            returned(c, o).wait_send()
        return carry

    lax.fori_loop(0, NCHUNK, drained, 0)


def scratch():
    v = pltpu.VMEM
    return [
        v((ROWS, D), BF16), v((D, HID), BF16), v((CH, HID), BF16), v((HID, LANE), BF16), v((LANE, HID), BF16),
        v((POOL, FEAT), BF16), v((1, NPATCH), jnp.int32), v((1, NPATCH), jnp.int32),
        v((ROWS, HID), F32), v((ROWS, HID), BF16), v((NCHUNK, MEMBERS, PATCH, LANE), F32),
        v((MEMBERS, NCHUNK, PATCH, LANE), F32), v((NPATCH, FEAT), BF16), v((ROWS, LANE), F32),
        v((ROWS, LANE), F32), v((ROWS, LANE), F32), v((len(PAIRS), 8, LANE), F32), v((len(PAIRS), LANE), F32),
        v((NCHUNK, MEMBERS, PATCH, LANE), F32), v((NCHUNK, MEMBERS, PATCH, LANE), F32),
        v((ROWS, LANE), BF16), v((ROWS, HID), BF16), v((D, ROWS), BF16), v((HID, ROWS), BF16),
        v((D, HID), F32), v((HID, LANE), F32),
        v((2, 4, 4, 8, 8, 256), F32), v((2, 4, 4, 8, 8, 256), F32), v((2, 8, 4, 2, 8, 128), F32),
        v((1, 4, 4, 8, 8, 256), F32), v((1, 4, 4, 8, 8, 256), F32), v((1, 8, 4, 2, 8, 128), F32),
        v((3, 4, 8, 8, 256), F32), v((3, 4, 8, 8, 256), F32), v((7, 4, 2, 8, 128), F32),
        v((3, 8, 8, 256), F32), v((3, 8, 8, 256), F32), v((3, 2, 8, 128), F32),
        v((7, 8, 256), F32), v((7, 8, 256), F32), v((3, 8, 128), F32),
        pltpu.SemaphoreType.DMA((9,)),
        pltpu.SemaphoreType.DMA((NCHUNK, MEMBERS)), pltpu.SemaphoreType.DMA((NCHUNK, MEMBERS)),
        pltpu.SemaphoreType.DMA((NCHUNK, MEMBERS)), pltpu.SemaphoreType.DMA((NCHUNK, MEMBERS)),
        pltpu.SemaphoreType.DMA((45,)), pltpu.SemaphoreType.DMA((45,)),
    ]


def unpack(packed, out1, out2):
    for i in range(2):
        value = packed[:, i * 256 : i * 256 + 256]
        out1[:, i * 512 : i * 512 + 256] = value[:4]
        out1[:, i * 512 + 256 : i * 512 + 512] = pltpu.roll(value, 4, 0)[:4]
    out2[...] = packed[:4, 512 : 512 + CH]


def shards(latent, w_in, w_out, observed, patch_index, counts):
    packed = pl.pallas_call(
        kernel,
        out_shape=jax.ShapeDtypeStruct((8, 640), F32),
        in_specs=[pl.BlockSpec(memory_space=pl.ANY)] * 6,
        out_specs=pl.BlockSpec(memory_space=pltpu.VMEM),
        scratch_shapes=scratch(),
        compiler_params=pltpu.CompilerParams(
            collective_id=0, has_side_effects=True, vmem_limit_bytes=60 * 1024 * 1024
        ),
    )(latent, w_in, w_out.T, observed, patch_index, counts)
    return pl.pallas_call(
        unpack,
        out_shape=(jax.ShapeDtypeStruct((4, HID), F32), jax.ShapeDtypeStruct((4, CH), F32)),
    )(packed)


def solution(mesh):
    placed = (
        P("member", "batch", "tile", None),
        P(),
        P(),
        P("batch", "tile", None),
        P("batch", "tile"),
        P("batch", "tile"),
    )
    rows = P(("member", "tile", "batch"), None)
    return jax.shard_map(
        shards, mesh=mesh, in_specs=placed, out_specs=(rows, rows), check_vma=False
    )
```

```python
import jax
import jax.numpy as jnp
from jax import lax
from jax.experimental import pallas as pl
from jax.experimental.pallas import tpu as pltpu
from jax.sharding import PartitionSpec as P

MESH = pl.DeviceIdType.MESH
F32, BF16 = jnp.float32, jnp.bfloat16
ROWS, D, HID, CH, LANE = 1024, 1024, 1024, 112, 128
PATCH, NPATCH, MEMBERS, POOL, FEAT = 16, 64, 16, 128, 1792
NCHUNK, CROWS = 4, 256
SLOTS = 96
ORDER = (1, 15, 2, 14, 3, 13, 4, 12, 5, 11, 6, 10, 7, 9, 8)
PAIRS = [(i, k) for i in range(MEMBERS) for k in range(i + 1, MEMBERS)]
PAIR_AT = {pair: at for at, pair in enumerate(PAIRS)}


def forward_chunk(c, lat, w_in, wo, pre, hid, dec):
    rows = pl.ds(pl.multiple_of(c * CROWS, CROWS), CROWS)
    v = jnp.dot(lat[rows, :], w_in[...], preferred_element_type=F32)
    pre[rows, :] = v
    hid[rows, :] = (v * (1.0 / (1.0 + jnp.exp(-v)))).astype(BF16)
    out = jnp.dot(hid[rows, :], wo[...], preferred_element_type=F32)
    dec[c] = out.reshape(MEMBERS, PATCH, LANE)


def slopes(pre):
    def step(i, carry):
        rows = pl.ds(pl.multiple_of(i * 64, 64), 64)
        v = pre[rows, :]
        sigma = 1.0 / (1.0 + jnp.exp(-v))
        pre[rows, :] = sigma * (1.0 + v * (1.0 - sigma))
        return carry

    lax.fori_loop(0, ROWS // 64, step, 0)


def transposed(src, dst):
    def step(i, carry):
        at = pl.ds(pl.multiple_of(i * 128, 128), 128)
        dst[at, :] = src[:, at].T
        return carry

    lax.fori_loop(0, 8, step, 0)


def own_term(obs, idx, cnt, dec, tgt, target, own, weight):
    pool_at = lax.broadcasted_iota(jnp.int32, (POOL, NPATCH), 0)
    choose = (pool_at == idx[...]).astype(F32).astype(BF16)
    picked = lax.dot_general(choose, obs[...], (((0,), (0,)), ((), ())), preferred_element_type=F32)
    tgt[...] = picked.astype(BF16)
    entry = lax.broadcasted_iota(jnp.int32, (256, LANE), 0)
    lane = lax.broadcasted_iota(jnp.int32, (256, LANE), 1)
    for i in range(PATCH):
        start = min(CH * i // 128 * 128, FEAT - 256)
        shift = ((entry == lane + (CH * i - start)) & (lane < CH)).astype(F32).astype(BF16)
        one = jnp.dot(tgt[:, start : start + 256], shift, preferred_element_type=F32)
        target[pl.ds(i, NPATCH, stride=PATCH), :] = one
    counts = cnt[...].astype(F32)

    def step(c, carry):
        rows = pl.ds(pl.multiple_of(c * CROWS, CROWS), CROWS)
        patch_of = (lax.broadcasted_iota(jnp.int32, (CROWS, NPATCH), 0) + c * CROWS) // PATCH
        at = lax.broadcasted_iota(jnp.int32, (CROWS, NPATCH), 1)
        count = jnp.sum(jnp.where(patch_of == at, counts, 0.0), axis=1, keepdims=True)
        delta = dec[c].reshape(CROWS, LANE) - target[rows, :]
        square = jnp.sum((delta * delta).reshape(MEMBERS, PATCH, LANE), axis=(1, 2), keepdims=True)
        scale = (1.0 / (MEMBERS * jnp.sqrt(square + 1.0))) * jnp.ones((MEMBERS, PATCH, LANE), F32)
        own[rows, :] = delta * scale.reshape(CROWS, LANE) * count
        weight[rows, :] = jnp.broadcast_to(count * (1.0 / (MEMBERS * MEMBERS)), (CROWS, LANE))
        return carry

    lax.fori_loop(0, NCHUNK, step, 0)


def pair_patch(c, x, part, inv, out):
    xs = [x[k, c] for k in range(MEMBERS)]
    for at, (i, k) in enumerate(PAIRS):
        d = xs[i] - xs[k]
        d = d * d
        part[at] = d[:8] + d[8:]
    total = jnp.sum(jnp.sum(part[...], axis=1), axis=1, keepdims=True)
    inv[...] = jnp.broadcast_to(1.0 / jnp.sqrt(total + 1.0), inv.shape)
    for i in range(MEMBERS):
        acc = None
        for k in range(MEMBERS):
            if k == i:
                continue
            at = PAIR_AT[(min(i, k), max(i, k))]
            term = (xs[i] - xs[k]) * inv[at : at + 1, :]
            acc = term if acc is None else acc + term
        out[c, i] = acc


def backward_chunk(c, back, own, weight, wo_t, slope, go, gp):
    rows = pl.ds(pl.multiple_of(c * CROWS, CROWS), CROWS)
    pair = back[c].reshape(CROWS, LANE)
    grad = (own[rows, :] - weight[rows, :] * pair).astype(BF16)
    go[rows, :] = grad
    gh = jnp.dot(grad, wo_t[...], preferred_element_type=F32)
    gp[rows, :] = (gh * slope[rows, :]).astype(BF16)


def accumulate(c, left, right, total):
    rows = pl.ds(pl.multiple_of(c * CROWS, CROWS), CROWS)

    def step(i, carry):
        at = pl.ds(pl.multiple_of(i * 256, 256), 256)
        total[at, :] += jnp.dot(left[at, rows], right[rows, :], preferred_element_type=F32)
        return carry

    lax.fori_loop(0, 4, step, 0)


def halves(lo, hi):
    top = lax.broadcasted_iota(jnp.int32, lo.shape, lo.ndim - 2) < 4
    axis = lo.ndim - 2
    return jnp.where(top, lo, pltpu.roll(hi, 4, axis)), jnp.where(top, pltpu.roll(lo, 4, axis), hi)


def last_chunk(left, right, total, i):
    rows = slice((NCHUNK - 1) * CROWS, NCHUNK * CROWS)
    at = slice(i * 256, i * 256 + 256)
    g = total[at, :] + jnp.dot(left[at, rows], right[rows, :], preferred_element_type=F32)
    return g.reshape(2, 2, 4, 2, 8, g.shape[1])


def kernel(
    lat_hbm, w_in_hbm, w_out_hbm, obs_hbm, idx_hbm, cnt_hbm, out,
    lat, w_in, w_raw, wo, wo_t, obs, idx, cnt, pre, hid, dec, x, tgt, target, own, weight, part, inv, ret, back,
    go, gp, lat_t, hid_t, sum1, sum2, qa, qb, qc,
    a0, b0, c0, ah, bh, c1, an, bn, af, bf, a2, b2, c2, a3, b3, c3,
    load_sem, there_send, there_recv, back_send, back_recv, rs_send, rs_recv,
):
    m, t, b = lax.axis_index("member"), lax.axis_index("tile"), lax.axis_index("batch")
    z, y_lo, xx, core = m // 2, m % 2, t // 2, t % 2
    y = b * 2 + y_lo

    def at_x(o):
        return {"tile": (xx + o) % 4 * 2 + core}

    def at_y(o):
        to = (y + o) % 4
        return {"member": z * 2 + to % 2, "batch": to // 2}

    def at_z(o):
        return {"member": (z + o) % 8 * 2 + y_lo}

    def at_member(o):
        return {"member": (m + o) % MEMBERS}

    def at_core():
        return {"tile": xx * 2 + (1 - core)}

    barrier = pltpu.get_barrier_semaphore()
    peers = [at_member(o) for o in range(1, 16)] + [at_core()] + [at_x(o) for o in range(1, 4)]
    for peer in peers:
        pl.semaphore_signal(barrier, inc=1, device_id=peer, device_id_type=MESH)
    for o in (1, 2, 3):
        pl.semaphore_signal(barrier, inc=1, device_id=at_y(o), device_id_type=MESH)

    def load_lat(c):
        rows = pl.ds(pl.multiple_of(c * CROWS, CROWS), CROWS)
        return pltpu.make_async_copy(lat_hbm.at[0, 0, rows, :], lat.at[rows, :], load_sem.at[c])

    load_w = pltpu.make_async_copy(w_in_hbm, w_in, load_sem.at[4])
    load_wo = pltpu.make_async_copy(w_out_hbm, w_raw, load_sem.at[5])
    later = [
        pltpu.make_async_copy(obs_hbm.at[0], obs, load_sem.at[6]),
        pltpu.make_async_copy(idx_hbm, idx, load_sem.at[7]),
        pltpu.make_async_copy(cnt_hbm, cnt, load_sem.at[8]),
    ]
    load_wo.start()
    load_w.start()
    for c in range(NCHUNK):
        load_lat(c).start()
    for load in later:
        load.start()
    wo_t[CH:, :] = jnp.zeros((LANE - CH, HID), BF16)
    load_wo.wait()
    wo_t[:CH, :] = w_raw[...]
    wo[...] = wo_t[...].T
    load_w.wait()

    def there(c, o):
        return pltpu.make_async_remote_copy(
            src_ref=dec.at[c, (m + o) % MEMBERS], dst_ref=x.at[m, c],
            send_sem=there_send.at[c, o], recv_sem=there_recv.at[c, o],
            device_id=at_member(o), device_id_type=MESH,
        )

    def returned(c, o):
        return pltpu.make_async_remote_copy(
            src_ref=ret.at[c, (m + o) % MEMBERS], dst_ref=back.at[c, m],
            send_sem=back_send.at[c, o], recv_sem=back_recv.at[c, o],
            device_id=at_member(o), device_id_type=MESH,
        )

    def arrived(make, c):
        for o in range(1, MEMBERS):
            make(c, o).wait_recv()

    def forward(c, carry):
        load_lat(c).wait()
        forward_chunk(c, lat, w_in, wo, pre, hid, dec)
        return carry

    def depart(c):
        x[m, c] = dec[c, m]
        for o in ORDER:
            there(c, o).start()

    def forward_and_depart(c, carry):
        forward(c, carry)
        depart(c)
        return carry

    forward(0, 0)
    pl.semaphore_wait(barrier, len(peers) + 3)
    depart(0)
    lax.fori_loop(1, NCHUNK, forward_and_depart, 0)

    for load in later:
        load.wait()
    own_term(obs, idx, cnt, dec, tgt, target, own, weight)
    slopes(pre)
    transposed(hid, hid_t)
    transposed(lat, lat_t)
    sum1[...] = jnp.zeros(sum1.shape, F32)
    sum2[...] = jnp.zeros(sum2.shape, F32)

    def score(c, carry):
        arrived(there, c)
        pair_patch(c, x, part, inv, ret)
        back[c, m] = ret[c, m]
        for o in ORDER:
            returned(c, o).start()
        return carry

    lax.fori_loop(0, NCHUNK, score, 0)

    def backward(c, carry):
        arrived(returned, c)
        backward_chunk(c, back, own, weight, wo_t, pre, go, gp)
        accumulate(c, hid_t, go, sum2)
        accumulate(c, lat_t, gp, sum1)
        return carry

    lax.fori_loop(0, NCHUNK - 1, backward, 0)
    arrived(returned, NCHUNK - 1)
    backward_chunk(NCHUNK - 1, back, own, weight, wo_t, pre, go, gp)

    slots = iter(range(SLOTS))
    sent = []

    def send(src, dst, device):
        at = next(slots)
        copy = pltpu.make_async_remote_copy(
            src_ref=src, dst_ref=dst, send_sem=rs_send.at[at], recv_sem=rs_recv.at[at],
            device_id=device, device_id_type=MESH,
        )
        copy.start()
        sent.append(copy)
        return copy

    def added(own_ref, landed, copies):
        for copy in copies:
            copy.wait_recv()
        total = own_ref[...]
        for ref in landed:
            total = total + ref[...]
        own_ref[...] = total

    class Group:
        def __init__(self, q, core_in, hop_in, near_in, far_in, second_in, third_in, at_p, at_q, p, q_at):
            self.q, self.core_in, self.hop_in, self.near_in, self.far_in = q, core_in, hop_in, near_in, far_in
            self.second_in, self.third_in, self.at_p, self.at_q = second_in, third_in, at_p, at_q
            self.p, self.q_at = p, q_at
            self.core_copy, self.hop, self.near, self.far, self.second = {}, {}, {}, {}, {}

        def part(self, to, h, k):
            return self.q.at[core, to, pl.ds(2 * h, 2), pl.ds(2 * k, 2)]

        def exchange(self, k):
            self.core_copy[k] = send(
                self.q.at[1 - core, :, :, pl.ds(2 * k, 2)], self.core_in.at[k], at_core()
            )

        def first(self, k):
            added(self.q.at[core, :, :, pl.ds(2 * k, 2)], [self.core_in.at[k]], [self.core_copy[k]])
            for h, s in ((0, 1), (1, 3)):
                self.hop[k, h] = send(self.part((self.p + 2) % 4, h, k), self.hop_in.at[k, h], self.at_p(s))
            for h, s in ((0, 1), (1, 3)):
                back_to = 4 - s
                self.near[k, h] = send(
                    self.part((self.p + back_to) % 4, h, k), self.near_in.at[k, h], self.at_p(back_to)
                )

        def relay(self, k):
            for h, s in ((0, 1), (1, 3)):
                added(self.hop_in.at[k, h], [self.part((self.p + s) % 4, h, k)], [self.hop[k, h]])
                self.far[k, h] = send(self.hop_in.at[k, h], self.far_in.at[k, h], self.at_p(s))

        def finish(self, k):
            for h in range(2):
                added(
                    self.part(self.p, h, k), [self.near_in.at[k, h], self.far_in.at[k, h]],
                    [self.near[k, h], self.far[k, h]],
                )

        def other_ring(self, i):
            zs = pl.ds(4 * i, 4)
            self.second[i] = [
                send(self.q.at[core, self.p, (self.q_at + o) % 4, zs], self.second_in.at[i, o - 1], self.at_q(o))
                for o in (2, 1, 3)
            ]

        def collect(self, i):
            landed = [self.second_in.at[i, o] for o in range(3)]
            added(self.q.at[core, self.p, self.q_at, pl.ds(4 * i, 4)], landed, self.second[i])

        def along_z(self):
            self.third = [
                send(self.q.at[core, self.p, self.q_at, (z + o) % 8], self.third_in.at[o - 1], at_z(o))
                for o in (4, 3, 5, 2, 6, 1, 7)
            ]

        def result(self):
            return last(self.q[core, self.p, self.q_at, z], self.third_in, self.third)

    def last(value, landed, copies):
        for copy in copies:
            copy.wait_recv()
        for j in range(landed.shape[0]):
            value = value + landed[j]
        return value

    ga = Group(qa, a0, ah, an, af, a2, a3, at_x, at_y, xx, y)
    gb = Group(qb, b0, bh, bn, bf, b2, b3, at_y, at_x, y, xx)
    both = (ga, gb)

    def product(k):
        g = last_chunk(lat_t, gp, sum1, k)
        for j in range(2):
            a_lo, a_hi = halves(g[j, ..., :256], g[j, ..., 256:512])
            b_lo, b_hi = halves(g[j, ..., 512:768], g[j, ..., 768:])
            for lo in range(2):
                for x_ in range(4):
                    for core_ in range(2):
                        qa[core_, x_, lo, 2 * k + j] = a_lo[lo, x_, core_]
                        qa[core_, x_, 2 + lo, 2 * k + j] = a_hi[lo, x_, core_]
                        qb[core_, lo, x_, 2 * k + j] = b_lo[lo, x_, core_]
                        qb[core_, 2 + lo, x_, 2 * k + j] = b_hi[lo, x_, core_]
        for group in both:
            group.exchange(k)

    def each(name, i):
        for group in both:
            getattr(group, name)(i)

    for k in range(4):
        g = last_chunk(hid_t, go, sum2, k)
        for j in range(2):
            c_lo, c_hi = halves(g[j, 0], g[j, 1])
            for x_ in range(4):
                for core_ in range(2):
                    qc[core_, 2 * k + j, x_, 0] = c_lo[x_, core_]
                    qc[core_, 2 * k + j, x_, 1] = c_hi[x_, core_]
    c_core = send(qc.at[1 - core], c0, at_core())
    product(0)
    product(1)
    added(qc.at[core], [c0], [c_core])
    c_one = [send(qc.at[core, (z + o) % 8], c1.at[o - 1], at_z(o)) for o in (4, 3, 5, 2, 6, 1, 7)]
    each("first", 0)
    product(2)
    each("first", 1)
    product(3)
    each("relay", 0)
    each("first", 2)
    each("relay", 1)
    each("first", 3)
    each("relay", 2)
    each("relay", 3)
    each("finish", 0)
    each("finish", 1)
    each("other_ring", 0)
    added(qc.at[core, z], [c1.at[j] for j in range(7)], c_one)
    c_two = [send(qc.at[core, z, (xx + o) % 4], c2.at[o - 1], at_x(o)) for o in (2, 1, 3)]
    each("finish", 2)
    each("finish", 3)
    each("other_ring", 1)
    added(qc.at[core, z, xx], [c2.at[j] for j in range(3)], c_two)
    c_three = [send(qc.at[core, z, xx, (y + o) % 4 // 2], c3.at[o - 1], at_y(o)) for o in (2, 1, 3)]
    each("collect", 0)
    each("collect", 1)
    for group in both:
        group.along_z()
    total = last(qc[core, z, xx, b], c3, c_three)
    out[:, 512:] = jnp.where(y_lo == 0, total, pltpu.roll(total, 4, 0))
    out[:, :256] = ga.result()
    out[:, 256:512] = gb.result()

    for copy in sent:
        copy.wait_send()

    def drained(c, carry):
        for o in range(1, MEMBERS):
            there(c, o).wait_send()
            returned(c, o).wait_send()
        return carry

    lax.fori_loop(0, NCHUNK, drained, 0)


def scratch():
    v = pltpu.VMEM
    return [
        v((ROWS, D), BF16), v((D, HID), BF16), v((CH, HID), BF16), v((HID, LANE), BF16), v((LANE, HID), BF16),
        v((POOL, FEAT), BF16), v((1, NPATCH), jnp.int32), v((1, NPATCH), jnp.int32),
        v((ROWS, HID), F32), v((ROWS, HID), BF16), v((NCHUNK, MEMBERS, PATCH, LANE), F32),
        v((MEMBERS, NCHUNK, PATCH, LANE), F32), v((NPATCH, FEAT), BF16), v((ROWS, LANE), F32),
        v((ROWS, LANE), F32), v((ROWS, LANE), F32), v((len(PAIRS), 8, LANE), F32), v((len(PAIRS), LANE), F32),
        v((NCHUNK, MEMBERS, PATCH, LANE), F32), v((NCHUNK, MEMBERS, PATCH, LANE), F32),
        v((ROWS, LANE), BF16), v((ROWS, HID), BF16), v((D, ROWS), BF16), v((HID, ROWS), BF16),
        v((D, HID), F32), v((HID, LANE), F32),
        v((2, 4, 4, 8, 8, 256), F32), v((2, 4, 4, 8, 8, 256), F32), v((2, 8, 4, 2, 8, 128), F32),
        v((4, 4, 4, 2, 8, 256), F32), v((4, 4, 4, 2, 8, 256), F32), v((8, 4, 2, 8, 128), F32),
        v((4, 2, 2, 2, 8, 256), F32), v((4, 2, 2, 2, 8, 256), F32), v((7, 4, 2, 8, 128), F32),
        v((4, 2, 2, 2, 8, 256), F32), v((4, 2, 2, 2, 8, 256), F32),
        v((4, 2, 2, 2, 8, 256), F32), v((4, 2, 2, 2, 8, 256), F32),
        v((2, 3, 4, 8, 256), F32), v((2, 3, 4, 8, 256), F32), v((3, 2, 8, 128), F32),
        v((7, 8, 256), F32), v((7, 8, 256), F32), v((3, 8, 128), F32),
        pltpu.SemaphoreType.DMA((9,)),
        pltpu.SemaphoreType.DMA((NCHUNK, MEMBERS)), pltpu.SemaphoreType.DMA((NCHUNK, MEMBERS)),
        pltpu.SemaphoreType.DMA((NCHUNK, MEMBERS)), pltpu.SemaphoreType.DMA((NCHUNK, MEMBERS)),
        pltpu.SemaphoreType.DMA((SLOTS,)), pltpu.SemaphoreType.DMA((SLOTS,)),
    ]


def unpack(packed, out1, out2):
    for i in range(2):
        value = packed[:, i * 256 : i * 256 + 256]
        out1[:, i * 512 : i * 512 + 256] = value[:4]
        out1[:, i * 512 + 256 : i * 512 + 512] = pltpu.roll(value, 4, 0)[:4]
    out2[...] = packed[:4, 512 : 512 + CH]


def shards(latent, w_in, w_out, observed, patch_index, counts):
    packed = pl.pallas_call(
        kernel,
        out_shape=jax.ShapeDtypeStruct((8, 640), F32),
        in_specs=[pl.BlockSpec(memory_space=pl.ANY)] * 6,
        out_specs=pl.BlockSpec(memory_space=pltpu.VMEM),
        scratch_shapes=scratch(),
        compiler_params=pltpu.CompilerParams(
            collective_id=0, has_side_effects=True, vmem_limit_bytes=60 * 1024 * 1024
        ),
    )(latent, w_in, w_out.T, observed, patch_index, counts)
    return pl.pallas_call(
        unpack,
        out_shape=(jax.ShapeDtypeStruct((4, HID), F32), jax.ShapeDtypeStruct((4, CH), F32)),
    )(packed)


def solution(mesh):
    placed = (
        P("member", "batch", "tile", None),
        P(),
        P(),
        P("batch", "tile", None),
        P("batch", "tile"),
        P("batch", "tile"),
    )
    rows = P(("member", "tile", "batch"), None)
    return jax.shard_map(
        shards, mesh=mesh, in_specs=placed, out_specs=(rows, rows), check_vma=False
    )
```

```python
import jax
import jax.numpy as jnp
from jax import lax
from jax.experimental import pallas as pl
from jax.experimental.pallas import tpu as pltpu
from jax.sharding import PartitionSpec as P

MESH = pl.DeviceIdType.MESH
F32, BF16 = jnp.float32, jnp.bfloat16
ROWS, D, HID, CH, LANE = 1024, 1024, 1024, 112, 128
PATCH, NPATCH, MEMBERS, POOL, FEAT = 16, 64, 16, 128, 1792
NCHUNK, CROWS = 4, 256
SLOTS = 96
VMEM_KIB = 55100
SENT = 14
ORDER = (1, 15, 2, 14, 3, 13, 4, 12, 5, 11, 6, 10, 7, 9, 8)
PAIRS = [(i, k) for i in range(MEMBERS) for k in range(i + 1, MEMBERS)]
PAIR_AT = {pair: at for at, pair in enumerate(PAIRS)}


def row_and_lane(shape):
    return lax.broadcasted_iota(jnp.int32, shape, 0), lax.broadcasted_iota(jnp.int32, shape, 1)


def pack_patch(value):
    row, lane = row_and_lane((PATCH, LANE))
    low = jnp.broadcast_to(value[14:15], (PATCH, LANE))
    high = pltpu.roll(jnp.broadcast_to(value[15:16], (PATCH, LANE)), 16, 1)
    moved = pltpu.roll(jnp.where(row < 7, low, high), 16, 1, stride=16, stride_axis=0)
    return jnp.where(row < SENT, jnp.where(lane < CH, value, moved), 0.0)


def unpack_patch(value):
    row, lane = row_and_lane((PATCH, LANE))
    moved = jnp.where((lane >= CH) & (row < SENT), value, 0.0)
    groups = jnp.where(row < 7, 7 - row, 14 - row)
    for bit in (4, 2, 1):
        moved = jnp.where((groups & bit) != 0, pltpu.roll(moved, 16 * bit, 1), moved)
    low = jnp.sum(jnp.where(row < 7, moved, 0.0), axis=0, keepdims=True)
    high = jnp.sum(jnp.where(row < 7, 0.0, moved), axis=0, keepdims=True)
    tail = jnp.where(row == 14, low, high)
    return jnp.where(row < SENT, jnp.where(lane < CH, value, 0.0), tail)


def forward_chunk(c, lat, w_in, wo, pre, hid, dec, packed):
    rows = pl.ds(pl.multiple_of(c * CROWS, CROWS), CROWS)
    v = jnp.dot(lat[rows, :], w_in[...], preferred_element_type=F32)
    pre[rows, :] = v
    hid[rows, :] = (v * (1.0 / (1.0 + jnp.exp(-v)))).astype(BF16)
    out = jnp.dot(hid[rows, :], wo[...], preferred_element_type=F32)
    dec[c] = out.reshape(MEMBERS, PATCH, LANE)
    for j in range(MEMBERS):
        packed[c, j] = pack_patch(out[j * PATCH : j * PATCH + PATCH])


def slopes(pre):
    def step(i, carry):
        rows = pl.ds(pl.multiple_of(i * 64, 64), 64)
        v = pre[rows, :]
        sigma = 1.0 / (1.0 + jnp.exp(-v))
        pre[rows, :] = sigma * (1.0 + v * (1.0 - sigma))
        return carry

    lax.fori_loop(0, ROWS // 64, step, 0)


def transposed(src, dst):
    def step(i, carry):
        at = pl.ds(pl.multiple_of(i * 128, 128), 128)
        dst[at, :] = src[:, at].T
        return carry

    lax.fori_loop(0, 8, step, 0)


def own_term(obs, idx, cnt, dec, tgt, target, own, weight):
    pool_at = lax.broadcasted_iota(jnp.int32, (POOL, NPATCH), 0)
    choose = (pool_at == idx[...]).astype(F32).astype(BF16)
    picked = lax.dot_general(choose, obs[...], (((0,), (0,)), ((), ())), preferred_element_type=F32)
    tgt[...] = picked.astype(BF16)
    entry = lax.broadcasted_iota(jnp.int32, (256, LANE), 0)
    lane = lax.broadcasted_iota(jnp.int32, (256, LANE), 1)
    for i in range(PATCH):
        start = min(CH * i // 128 * 128, FEAT - 256)
        shift = ((entry == lane + (CH * i - start)) & (lane < CH)).astype(F32).astype(BF16)
        one = jnp.dot(tgt[:, start : start + 256], shift, preferred_element_type=F32)
        target[pl.ds(i, NPATCH, stride=PATCH), :] = one
    counts = cnt[...].astype(F32)

    def step(c, carry):
        rows = pl.ds(pl.multiple_of(c * CROWS, CROWS), CROWS)
        patch_of = (lax.broadcasted_iota(jnp.int32, (CROWS, NPATCH), 0) + c * CROWS) // PATCH
        at = lax.broadcasted_iota(jnp.int32, (CROWS, NPATCH), 1)
        count = jnp.sum(jnp.where(patch_of == at, counts, 0.0), axis=1, keepdims=True)
        delta = dec[c].reshape(CROWS, LANE) - target[rows, :]
        square = jnp.sum((delta * delta).reshape(MEMBERS, PATCH, LANE), axis=(1, 2), keepdims=True)
        scale = (1.0 / (MEMBERS * jnp.sqrt(square + 1.0))) * jnp.ones((MEMBERS, PATCH, LANE), F32)
        own[rows, :] = delta * scale.reshape(CROWS, LANE) * count
        weight[rows, :] = jnp.broadcast_to(count * (1.0 / (MEMBERS * MEMBERS)), (CROWS, LANE))
        return carry

    lax.fori_loop(0, NCHUNK, step, 0)


def pair_patch(c, x, part, inv, out):
    xs = [x[k, c] for k in range(MEMBERS)]
    for at, (i, k) in enumerate(PAIRS):
        d = xs[i] - xs[k]
        d = d * d
        part[at] = d[:8] + d[8:]
    total = jnp.sum(jnp.sum(part[...], axis=1), axis=1, keepdims=True)
    inv[...] = jnp.broadcast_to(1.0 / jnp.sqrt(total + 1.0), inv.shape)
    for i in range(MEMBERS):
        acc = None
        for k in range(MEMBERS):
            if k == i:
                continue
            at = PAIR_AT[(min(i, k), max(i, k))]
            term = (xs[i] - xs[k]) * inv[at : at + 1, :]
            acc = term if acc is None else acc + term
        out[c, i] = acc


def backward_chunk(c, back, own, weight, wo_t, slope, go, gp):
    rows = pl.ds(pl.multiple_of(c * CROWS, CROWS), CROWS)
    pair = jnp.concatenate([unpack_patch(back[c, j]) for j in range(MEMBERS)], axis=0)
    grad = (own[rows, :] - weight[rows, :] * pair).astype(BF16)
    go[rows, :] = grad
    gh = jnp.dot(grad, wo_t[...], preferred_element_type=F32)
    gp[rows, :] = (gh * slope[rows, :]).astype(BF16)


def accumulate(c, left, right, total):
    rows = pl.ds(pl.multiple_of(c * CROWS, CROWS), CROWS)

    def step(i, carry):
        at = pl.ds(pl.multiple_of(i * 256, 256), 256)
        total[at, :] += jnp.dot(left[at, rows], right[rows, :], preferred_element_type=F32)
        return carry

    lax.fori_loop(0, 4, step, 0)


def halves(lo, hi):
    top = lax.broadcasted_iota(jnp.int32, lo.shape, lo.ndim - 2) < 4
    axis = lo.ndim - 2
    return jnp.where(top, lo, pltpu.roll(hi, 4, axis)), jnp.where(top, pltpu.roll(lo, 4, axis), hi)


def last_chunk(left, right, total, i):
    rows = slice((NCHUNK - 1) * CROWS, NCHUNK * CROWS)
    at = slice(i * 256, i * 256 + 256)
    g = total[at, :] + jnp.dot(left[at, rows], right[rows, :], preferred_element_type=F32)
    return g.reshape(2, 2, 4, 2, 8, g.shape[1])


def kernel(
    lat_hbm, w_in_hbm, w_out_hbm, obs_hbm, idx_hbm, cnt_hbm, out,
    lat, w_in, w_raw, wo, wo_t, obs, idx, cnt, pre, hid, dec, packed, x, tgt, target, own, weight, part, inv, ret, back,
    go, gp, lat_t, hid_t, sum1, sum2, qa, qb, qc,
    a0, b0, c0, ah, bh, c1, an, bn, af, bf, a2, b2, c2, a3, b3, c3,
    load_sem, there_send, there_recv, back_send, back_recv, rs_send, rs_recv,
):
    m, t, b = lax.axis_index("member"), lax.axis_index("tile"), lax.axis_index("batch")
    z, y_lo, xx, core = m // 2, m % 2, t // 2, t % 2
    y = b * 2 + y_lo

    def at_x(o):
        return {"tile": (xx + o) % 4 * 2 + core}

    def at_y(o):
        to = (y + o) % 4
        return {"member": z * 2 + to % 2, "batch": to // 2}

    def at_z(o):
        return {"member": (z + o) % 8 * 2 + y_lo}

    def at_member(o):
        return {"member": (m + o) % MEMBERS}

    def at_core():
        return {"tile": xx * 2 + (1 - core)}

    x[...] = jnp.zeros(x.shape, F32)
    barrier = pltpu.get_barrier_semaphore()
    peers = [at_member(o) for o in range(1, 16)] + [at_core()] + [at_x(o) for o in range(1, 4)]
    for peer in peers:
        pl.semaphore_signal(barrier, inc=1, device_id=peer, device_id_type=MESH)
    for o in (1, 2, 3):
        pl.semaphore_signal(barrier, inc=1, device_id=at_y(o), device_id_type=MESH)

    def load_lat(c):
        rows = pl.ds(pl.multiple_of(c * CROWS, CROWS), CROWS)
        return pltpu.make_async_copy(lat_hbm.at[0, 0, rows, :], lat.at[rows, :], load_sem.at[c])

    load_w = pltpu.make_async_copy(w_in_hbm, w_in, load_sem.at[4])
    load_wo = pltpu.make_async_copy(w_out_hbm, w_raw, load_sem.at[5])
    later = [
        pltpu.make_async_copy(obs_hbm.at[0], obs, load_sem.at[6]),
        pltpu.make_async_copy(idx_hbm, idx, load_sem.at[7]),
        pltpu.make_async_copy(cnt_hbm, cnt, load_sem.at[8]),
    ]
    load_wo.start()
    load_w.start()
    for c in range(NCHUNK):
        load_lat(c).start()
    for load in later:
        load.start()
    wo_t[CH:, :] = jnp.zeros((LANE - CH, HID), BF16)
    load_wo.wait()
    wo_t[:CH, :] = w_raw[...]
    wo[...] = wo_t[...].T
    load_w.wait()

    def there(c, o):
        return pltpu.make_async_remote_copy(
            src_ref=packed.at[c, (m + o) % MEMBERS, pl.ds(0, SENT)], dst_ref=x.at[m, c, pl.ds(0, SENT)],
            send_sem=there_send.at[c, o], recv_sem=there_recv.at[c, o],
            device_id=at_member(o), device_id_type=MESH,
        )

    def returned(c, o):
        return pltpu.make_async_remote_copy(
            src_ref=ret.at[c, (m + o) % MEMBERS, pl.ds(0, SENT)], dst_ref=back.at[c, m, pl.ds(0, SENT)],
            send_sem=back_send.at[c, o], recv_sem=back_recv.at[c, o],
            device_id=at_member(o), device_id_type=MESH,
        )

    def arrived(make, c):
        for o in range(1, MEMBERS):
            make(c, o).wait_recv()

    def forward(c, carry):
        load_lat(c).wait()
        forward_chunk(c, lat, w_in, wo, pre, hid, dec, packed)
        return carry

    def depart(c):
        x[m, c] = packed[c, m]
        for o in ORDER:
            there(c, o).start()

    def forward_and_depart(c, carry):
        forward(c, carry)
        depart(c)
        return carry

    forward(0, 0)
    pl.semaphore_wait(barrier, len(peers) + 3)
    depart(0)
    lax.fori_loop(1, NCHUNK, forward_and_depart, 0)

    for load in later:
        load.wait()
    own_term(obs, idx, cnt, dec, tgt, target, own, weight)
    slopes(pre)
    transposed(hid, hid_t)
    transposed(lat, lat_t)
    sum1[...] = jnp.zeros(sum1.shape, F32)
    sum2[...] = jnp.zeros(sum2.shape, F32)

    def score(c, carry):
        arrived(there, c)
        pair_patch(c, x, part, inv, ret)
        back[c, m] = ret[c, m]
        for o in ORDER:
            returned(c, o).start()
        return carry

    lax.fori_loop(0, NCHUNK, score, 0)

    def backward(c, carry):
        arrived(returned, c)
        backward_chunk(c, back, own, weight, wo_t, pre, go, gp)
        accumulate(c, hid_t, go, sum2)
        accumulate(c, lat_t, gp, sum1)
        return carry

    lax.fori_loop(0, NCHUNK - 1, backward, 0)
    arrived(returned, NCHUNK - 1)
    backward_chunk(NCHUNK - 1, back, own, weight, wo_t, pre, go, gp)

    slots = iter(range(SLOTS))
    sent = []

    def send(src, dst, device):
        at = next(slots)
        copy = pltpu.make_async_remote_copy(
            src_ref=src, dst_ref=dst, send_sem=rs_send.at[at], recv_sem=rs_recv.at[at],
            device_id=device, device_id_type=MESH,
        )
        copy.start()
        sent.append(copy)
        return copy

    def added(own_ref, landed, copies):
        for copy in copies:
            copy.wait_recv()
        total = own_ref[...]
        for ref in landed:
            total = total + ref[...]
        own_ref[...] = total

    class Group:
        def __init__(self, q, core_in, hop_in, near_in, far_in, second_in, third_in, at_p, at_q, p, q_at):
            self.q, self.core_in, self.hop_in, self.near_in, self.far_in = q, core_in, hop_in, near_in, far_in
            self.second_in, self.third_in, self.at_p, self.at_q = second_in, third_in, at_p, at_q
            self.p, self.q_at = p, q_at
            self.core_copy, self.hop, self.near, self.far, self.second = {}, {}, {}, {}, {}

        def part(self, to, h, k):
            return self.q.at[core, to, pl.ds(2 * h, 2), pl.ds(2 * k, 2)]

        def exchange(self, k):
            self.core_copy[k] = send(
                self.q.at[1 - core, :, :, pl.ds(2 * k, 2)], self.core_in.at[k], at_core()
            )

        def first(self, k):
            added(self.q.at[core, :, :, pl.ds(2 * k, 2)], [self.core_in.at[k]], [self.core_copy[k]])
            for h, s in ((0, 1), (1, 3)):
                self.hop[k, h] = send(self.part((self.p + 2) % 4, h, k), self.hop_in.at[k, h], self.at_p(s))
            for h, s in ((0, 1), (1, 3)):
                back_to = 4 - s
                self.near[k, h] = send(
                    self.part((self.p + back_to) % 4, h, k), self.near_in.at[k, h], self.at_p(back_to)
                )

        def relay(self, k):
            for h, s in ((0, 1), (1, 3)):
                added(self.hop_in.at[k, h], [self.part((self.p + s) % 4, h, k)], [self.hop[k, h]])
                self.far[k, h] = send(self.hop_in.at[k, h], self.far_in.at[k, h], self.at_p(s))

        def finish(self, k):
            for h in range(2):
                added(
                    self.part(self.p, h, k), [self.near_in.at[k, h], self.far_in.at[k, h]],
                    [self.near[k, h], self.far[k, h]],
                )

        def other_ring(self, i):
            zs = pl.ds(4 * i, 4)
            self.second[i] = [
                send(self.q.at[core, self.p, (self.q_at + o) % 4, zs], self.second_in.at[i, o - 1], self.at_q(o))
                for o in (2, 1, 3)
            ]

        def collect(self, i):
            landed = [self.second_in.at[i, o] for o in range(3)]
            added(self.q.at[core, self.p, self.q_at, pl.ds(4 * i, 4)], landed, self.second[i])

        def along_z(self):
            self.third = [
                send(self.q.at[core, self.p, self.q_at, (z + o) % 8], self.third_in.at[o - 1], at_z(o))
                for o in (4, 3, 5, 2, 6, 1, 7)
            ]

        def result(self):
            return last(self.q[core, self.p, self.q_at, z], self.third_in, self.third)

    def last(value, landed, copies):
        for copy in copies:
            copy.wait_recv()
        for j in range(landed.shape[0]):
            value = value + landed[j]
        return value

    ga = Group(qa, a0, ah, an, af, a2, a3, at_x, at_y, xx, y)
    gb = Group(qb, b0, bh, bn, bf, b2, b3, at_y, at_x, y, xx)
    both = (ga, gb)

    def product(k):
        g = last_chunk(lat_t, gp, sum1, k)
        for j in range(2):
            a_lo, a_hi = halves(g[j, ..., :256], g[j, ..., 256:512])
            b_lo, b_hi = halves(g[j, ..., 512:768], g[j, ..., 768:])
            for lo in range(2):
                for x_ in range(4):
                    for core_ in range(2):
                        qa[core_, x_, lo, 2 * k + j] = a_lo[lo, x_, core_]
                        qa[core_, x_, 2 + lo, 2 * k + j] = a_hi[lo, x_, core_]
                        qb[core_, lo, x_, 2 * k + j] = b_lo[lo, x_, core_]
                        qb[core_, 2 + lo, x_, 2 * k + j] = b_hi[lo, x_, core_]
        for group in both:
            group.exchange(k)

    def each(name, i):
        for group in both:
            getattr(group, name)(i)

    for k in range(4):
        g = last_chunk(hid_t, go, sum2, k)
        for j in range(2):
            c_lo, c_hi = halves(g[j, 0], g[j, 1])
            for x_ in range(4):
                for core_ in range(2):
                    qc[core_, 2 * k + j, x_, 0] = c_lo[x_, core_]
                    qc[core_, 2 * k + j, x_, 1] = c_hi[x_, core_]
    c_core = send(qc.at[1 - core], c0, at_core())
    product(0)
    product(1)
    added(qc.at[core], [c0], [c_core])
    c_one = [send(qc.at[core, (z + o) % 8], c1.at[o - 1], at_z(o)) for o in (4, 3, 5, 2, 6, 1, 7)]
    each("first", 0)
    product(2)
    each("first", 1)
    product(3)
    each("relay", 0)
    each("first", 2)
    each("relay", 1)
    each("first", 3)
    each("relay", 2)
    each("relay", 3)
    each("finish", 0)
    each("finish", 1)
    each("other_ring", 0)
    added(qc.at[core, z], [c1.at[j] for j in range(7)], c_one)
    c_two = [send(qc.at[core, z, (xx + o) % 4], c2.at[o - 1], at_x(o)) for o in (2, 1, 3)]
    each("finish", 2)
    each("finish", 3)
    each("other_ring", 1)
    added(qc.at[core, z, xx], [c2.at[j] for j in range(3)], c_two)
    c_three = [send(qc.at[core, z, xx, (y + o) % 4 // 2], c3.at[o - 1], at_y(o)) for o in (2, 1, 3)]
    each("collect", 0)
    each("collect", 1)
    for group in both:
        group.along_z()
    total = last(qc[core, z, xx, b], c3, c_three)
    out[:, 512:] = jnp.where(y_lo == 0, total, pltpu.roll(total, 4, 0))
    out[:, :256] = ga.result()
    out[:, 256:512] = gb.result()

    for copy in sent:
        copy.wait_send()

    def drained(c, carry):
        for o in range(1, MEMBERS):
            there(c, o).wait_send()
            returned(c, o).wait_send()
        return carry

    lax.fori_loop(0, NCHUNK, drained, 0)


def scratch():
    v = pltpu.VMEM
    return [
        v((ROWS, D), BF16), v((D, HID), BF16), v((CH, HID), BF16), v((HID, LANE), BF16), v((LANE, HID), BF16),
        v((POOL, FEAT), BF16), v((1, NPATCH), jnp.int32), v((1, NPATCH), jnp.int32),
        v((ROWS, HID), F32), v((ROWS, HID), BF16), v((NCHUNK, MEMBERS, PATCH, LANE), F32), v((NCHUNK, MEMBERS, PATCH, LANE), F32),
        v((MEMBERS, NCHUNK, PATCH, LANE), F32), v((NPATCH, FEAT), BF16), v((ROWS, LANE), F32),
        v((ROWS, LANE), F32), v((ROWS, LANE), F32), v((len(PAIRS), 8, LANE), F32), v((len(PAIRS), LANE), F32),
        v((NCHUNK, MEMBERS, PATCH, LANE), F32), v((NCHUNK, MEMBERS, PATCH, LANE), F32),
        v((ROWS, LANE), BF16), v((ROWS, HID), BF16), v((D, ROWS), BF16), v((HID, ROWS), BF16),
        v((D, HID), F32), v((HID, LANE), F32),
        v((2, 4, 4, 8, 8, 256), F32), v((2, 4, 4, 8, 8, 256), F32), v((2, 8, 4, 2, 8, 128), F32),
        v((4, 4, 4, 2, 8, 256), F32), v((4, 4, 4, 2, 8, 256), F32), v((8, 4, 2, 8, 128), F32),
        v((4, 2, 2, 2, 8, 256), F32), v((4, 2, 2, 2, 8, 256), F32), v((7, 4, 2, 8, 128), F32),
        v((4, 2, 2, 2, 8, 256), F32), v((4, 2, 2, 2, 8, 256), F32),
        v((4, 2, 2, 2, 8, 256), F32), v((4, 2, 2, 2, 8, 256), F32),
        v((2, 3, 4, 8, 256), F32), v((2, 3, 4, 8, 256), F32), v((3, 2, 8, 128), F32),
        v((7, 8, 256), F32), v((7, 8, 256), F32), v((3, 8, 128), F32),
        pltpu.SemaphoreType.DMA((9,)),
        pltpu.SemaphoreType.DMA((NCHUNK, MEMBERS)), pltpu.SemaphoreType.DMA((NCHUNK, MEMBERS)),
        pltpu.SemaphoreType.DMA((NCHUNK, MEMBERS)), pltpu.SemaphoreType.DMA((NCHUNK, MEMBERS)),
        pltpu.SemaphoreType.DMA((SLOTS,)), pltpu.SemaphoreType.DMA((SLOTS,)),
    ]


def unpack(packed, out1, out2):
    for i in range(2):
        value = packed[:, i * 256 : i * 256 + 256]
        out1[:, i * 512 : i * 512 + 256] = value[:4]
        out1[:, i * 512 + 256 : i * 512 + 512] = pltpu.roll(value, 4, 0)[:4]
    out2[...] = packed[:4, 512 : 512 + CH]


def shards(latent, w_in, w_out, observed, patch_index, counts):
    packed = pl.pallas_call(
        kernel,
        out_shape=jax.ShapeDtypeStruct((8, 640), F32),
        in_specs=[pl.BlockSpec(memory_space=pl.ANY)] * 6,
        out_specs=pl.BlockSpec(memory_space=pltpu.VMEM),
        scratch_shapes=scratch(),
        compiler_params=pltpu.CompilerParams(
            collective_id=0, has_side_effects=True, vmem_limit_bytes=VMEM_KIB * 1024
        ),
    )(latent, w_in, w_out.T, observed, patch_index, counts)
    return pl.pallas_call(
        unpack,
        out_shape=(jax.ShapeDtypeStruct((4, HID), F32), jax.ShapeDtypeStruct((4, CH), F32)),
        compiler_params=pltpu.CompilerParams(vmem_limit_bytes=1024 * 1024),
    )(packed)


def solution(mesh):
    placed = (
        P("member", "batch", "tile", None),
        P(),
        P(),
        P("batch", "tile", None),
        P("batch", "tile"),
        P("batch", "tile"),
    )
    rows = P(("member", "tile", "batch"), None)
    return jax.shard_map(
        shards, mesh=mesh, in_specs=placed, out_specs=(rows, rows), check_vma=False
    )
```

```python
import jax
import jax.numpy as jnp
from jax import lax
from jax.experimental import pallas as pl
from jax.experimental.pallas import tpu as pltpu
from jax.sharding import PartitionSpec as P

MESH = pl.DeviceIdType.MESH
F32, BF16 = jnp.float32, jnp.bfloat16
ROWS, D, HID, CH, LANE = 1024, 1024, 1024, 112, 128
PATCH, NPATCH, MEMBERS, POOL, FEAT = 16, 64, 16, 128, 1792
NCHUNK, CROWS = 4, 256
SLOTS = 82
VMEM_KIB = 55100
SENT = 14
ORDER = (8, 7, 9, 6, 10, 5, 11, 4, 12, 3, 13, 2, 14, 1, 15)
PAIRS = [(i, k) for i in range(MEMBERS) for k in range(i + 1, MEMBERS)]
PAIR_AT = {pair: at for at, pair in enumerate(PAIRS)}


def row_and_lane(shape):
    return lax.broadcasted_iota(jnp.int32, shape, 0), lax.broadcasted_iota(jnp.int32, shape, 1)


def pack_patch(value):
    row, lane = row_and_lane((PATCH, LANE))
    low = jnp.broadcast_to(value[14:15], (PATCH, LANE))
    high = pltpu.roll(jnp.broadcast_to(value[15:16], (PATCH, LANE)), 16, 1)
    moved = pltpu.roll(jnp.where(row < 7, low, high), 16, 1, stride=16, stride_axis=0)
    return jnp.where(row < SENT, jnp.where(lane < CH, value, moved), 0.0)


def unpack_patch(value):
    row, lane = row_and_lane((PATCH, LANE))
    moved = jnp.where((lane >= CH) & (row < SENT), value, 0.0)
    groups = jnp.where(row < 7, 7 - row, 14 - row)
    for bit in (4, 2, 1):
        moved = jnp.where((groups & bit) != 0, pltpu.roll(moved, 16 * bit, 1), moved)
    low = jnp.sum(jnp.where(row < 7, moved, 0.0), axis=0, keepdims=True)
    high = jnp.sum(jnp.where(row < 7, 0.0, moved), axis=0, keepdims=True)
    tail = jnp.where(row == 14, low, high)
    return jnp.where(row < SENT, jnp.where(lane < CH, value, 0.0), tail)


def forward_chunk(c, lat, w_in, wo, pre, hid, dec, packed):
    rows = pl.ds(pl.multiple_of(c * CROWS, CROWS), CROWS)
    v = jnp.dot(lat[rows, :], w_in[...], preferred_element_type=F32)
    pre[rows, :] = v
    hid[rows, :] = (v * (1.0 / (1.0 + jnp.exp(-v)))).astype(BF16)
    out = jnp.dot(hid[rows, :], wo[...], preferred_element_type=F32)
    dec[c] = out.reshape(MEMBERS, PATCH, LANE)
    for j in range(MEMBERS):
        packed[c, j] = pack_patch(out[j * PATCH : j * PATCH + PATCH])


def slopes(pre):
    def step(i, carry):
        rows = pl.ds(pl.multiple_of(i * 64, 64), 64)
        v = pre[rows, :]
        sigma = 1.0 / (1.0 + jnp.exp(-v))
        pre[rows, :] = sigma * (1.0 + v * (1.0 - sigma))
        return carry

    lax.fori_loop(0, ROWS // 64, step, 0)


def transposed(src, dst):
    def step(i, carry):
        at = pl.ds(pl.multiple_of(i * 128, 128), 128)
        dst[at, :] = src[:, at].T
        return carry

    lax.fori_loop(0, 8, step, 0)


def own_term(obs, idx, cnt, dec, tgt, target, own, weight):
    pool_at = lax.broadcasted_iota(jnp.int32, (POOL, NPATCH), 0)
    choose = (pool_at == idx[...]).astype(F32).astype(BF16)
    picked = lax.dot_general(choose, obs[...], (((0,), (0,)), ((), ())), preferred_element_type=F32)
    tgt[...] = picked.astype(BF16)
    entry = lax.broadcasted_iota(jnp.int32, (256, LANE), 0)
    lane = lax.broadcasted_iota(jnp.int32, (256, LANE), 1)
    for i in range(PATCH):
        start = min(CH * i // 128 * 128, FEAT - 256)
        shift = ((entry == lane + (CH * i - start)) & (lane < CH)).astype(F32).astype(BF16)
        one = jnp.dot(tgt[:, start : start + 256], shift, preferred_element_type=F32)
        target[pl.ds(i, NPATCH, stride=PATCH), :] = one
    counts = cnt[...].astype(F32)

    def step(c, carry):
        rows = pl.ds(pl.multiple_of(c * CROWS, CROWS), CROWS)
        patch_of = (lax.broadcasted_iota(jnp.int32, (CROWS, NPATCH), 0) + c * CROWS) // PATCH
        at = lax.broadcasted_iota(jnp.int32, (CROWS, NPATCH), 1)
        count = jnp.sum(jnp.where(patch_of == at, counts, 0.0), axis=1, keepdims=True)
        delta = dec[c].reshape(CROWS, LANE) - target[rows, :]
        square = jnp.sum((delta * delta).reshape(MEMBERS, PATCH, LANE), axis=(1, 2), keepdims=True)
        scale = (1.0 / (MEMBERS * jnp.sqrt(square + 1.0))) * jnp.ones((MEMBERS, PATCH, LANE), F32)
        own[rows, :] = delta * scale.reshape(CROWS, LANE) * count
        weight[rows, :] = jnp.broadcast_to(count * (1.0 / (MEMBERS * MEMBERS)), (CROWS, LANE))
        return carry

    lax.fori_loop(0, NCHUNK, step, 0)


def pair_patch(c, x, part, inv, out):
    xs = [x[k, c] for k in range(MEMBERS)]
    for at, (i, k) in enumerate(PAIRS):
        d = xs[i] - xs[k]
        d = d * d
        part[at] = d[:8] + d[8:]
    total = jnp.sum(jnp.sum(part[...], axis=1), axis=1, keepdims=True)
    inv[...] = jnp.broadcast_to(1.0 / jnp.sqrt(total + 1.0), inv.shape)
    for i in range(MEMBERS):
        acc = None
        for k in range(MEMBERS):
            if k == i:
                continue
            at = PAIR_AT[(min(i, k), max(i, k))]
            term = (xs[i] - xs[k]) * inv[at : at + 1, :]
            acc = term if acc is None else acc + term
        out[c, i] = acc


def backward_chunk(c, back, own, weight, wo_t, slope, go, gp):
    rows = pl.ds(pl.multiple_of(c * CROWS, CROWS), CROWS)
    pair = jnp.concatenate([unpack_patch(back[c, j]) for j in range(MEMBERS)], axis=0)
    grad = (own[rows, :] - weight[rows, :] * pair).astype(BF16)
    go[rows, :] = grad
    gh = jnp.dot(grad, wo_t[...], preferred_element_type=F32)
    gp[rows, :] = (gh * slope[rows, :]).astype(BF16)


def accumulate(c, left, right, total):
    rows = pl.ds(pl.multiple_of(c * CROWS, CROWS), CROWS)

    def step(i, carry):
        at = pl.ds(pl.multiple_of(i * 256, 256), 256)
        total[at, :] += jnp.dot(left[at, rows], right[rows, :], preferred_element_type=F32)
        return carry

    lax.fori_loop(0, 4, step, 0)


def halves(lo, hi):
    top = lax.broadcasted_iota(jnp.int32, lo.shape, lo.ndim - 2) < 4
    axis = lo.ndim - 2
    return jnp.where(top, lo, pltpu.roll(hi, 4, axis)), jnp.where(top, pltpu.roll(lo, 4, axis), hi)


def last_chunk(left, right, total, i):
    rows = slice((NCHUNK - 1) * CROWS, NCHUNK * CROWS)
    at = slice(i * 256, i * 256 + 256)
    g = total[at, :] + jnp.dot(left[at, rows], right[rows, :], preferred_element_type=F32)
    return g.reshape(2, 2, 4, 2, 8, g.shape[1])


def kernel(
    lat_hbm, w_in_hbm, w_out_hbm, obs_hbm, idx_hbm, cnt_hbm, out,
    lat, w_in, w_raw, wo, wo_t, obs, idx, cnt, pre, hid, dec, packed, x, tgt, target, own, weight, part, inv, ret, back,
    go, gp, lat_t, hid_t, sum1, sum2, qa, qb, qc,
    a0, b0, c0, ah, bh, c1, an, bn, af, bf, a2, b2, c2, a3, b3, c3,
    load_sem, there_send, there_recv, back_send, back_recv, rs_send, rs_recv, za_send, za_recv, zb_send, zb_recv,
):
    m, t, b = lax.axis_index("member"), lax.axis_index("tile"), lax.axis_index("batch")
    z, y_lo, xx, core = m // 2, m % 2, t // 2, t % 2
    y = b * 2 + y_lo

    def at_x(o):
        return {"tile": (xx + o) % 4 * 2 + core}

    def at_y(o):
        to = (y + o) % 4
        return {"member": z * 2 + to % 2, "batch": to // 2}

    def at_z(o):
        return {"member": (z + o) % 8 * 2 + y_lo}

    def at_member(o):
        return {"member": (m + o) % MEMBERS}

    def at_core():
        return {"tile": xx * 2 + (1 - core)}

    x[...] = jnp.zeros(x.shape, F32)
    barrier = pltpu.get_barrier_semaphore()
    peers = [at_member(o) for o in range(1, 16)] + [at_core()] + [at_x(o) for o in range(1, 4)]
    for peer in peers:
        pl.semaphore_signal(barrier, inc=1, device_id=peer, device_id_type=MESH)
    for o in (1, 2, 3):
        pl.semaphore_signal(barrier, inc=1, device_id=at_y(o), device_id_type=MESH)

    def load_lat(c):
        rows = pl.ds(pl.multiple_of(c * CROWS, CROWS), CROWS)
        return pltpu.make_async_copy(lat_hbm.at[0, 0, rows, :], lat.at[rows, :], load_sem.at[c])

    load_w = pltpu.make_async_copy(w_in_hbm, w_in, load_sem.at[4])
    load_wo = pltpu.make_async_copy(w_out_hbm, w_raw, load_sem.at[5])
    later = [
        pltpu.make_async_copy(obs_hbm.at[0], obs, load_sem.at[6]),
        pltpu.make_async_copy(idx_hbm, idx, load_sem.at[7]),
        pltpu.make_async_copy(cnt_hbm, cnt, load_sem.at[8]),
    ]
    load_wo.start()
    load_w.start()
    for c in range(NCHUNK):
        load_lat(c).start()
    for load in later:
        load.start()
    wo_t[CH:, :] = jnp.zeros((LANE - CH, HID), BF16)
    load_wo.wait()
    wo_t[:CH, :] = w_raw[...]
    wo[...] = wo_t[...].T
    load_w.wait()

    def there(c, o):
        return pltpu.make_async_remote_copy(
            src_ref=packed.at[c, (m + o) % MEMBERS, pl.ds(0, SENT)], dst_ref=x.at[m, c, pl.ds(0, SENT)],
            send_sem=there_send.at[c, o], recv_sem=there_recv.at[c, o],
            device_id=at_member(o), device_id_type=MESH,
        )

    def returned(c, o):
        return pltpu.make_async_remote_copy(
            src_ref=ret.at[c, (m + o) % MEMBERS, pl.ds(0, SENT)], dst_ref=back.at[c, m, pl.ds(0, SENT)],
            send_sem=back_send.at[c, o], recv_sem=back_recv.at[c, o],
            device_id=at_member(o), device_id_type=MESH,
        )

    def arrived(make, c):
        for o in range(1, MEMBERS):
            make(c, o).wait_recv()

    def forward(c, carry):
        load_lat(c).wait()
        forward_chunk(c, lat, w_in, wo, pre, hid, dec, packed)
        return carry

    def depart(c):
        x[m, c] = packed[c, m]
        for o in ORDER:
            there(c, o).start()

    def forward_and_depart(c, carry):
        forward(c, carry)
        depart(c)
        return carry

    forward(0, 0)
    pl.semaphore_wait(barrier, len(peers) + 3)
    depart(0)
    lax.fori_loop(1, NCHUNK, forward_and_depart, 0)

    for load in later:
        load.wait()
    own_term(obs, idx, cnt, dec, tgt, target, own, weight)
    slopes(pre)
    transposed(hid, hid_t)
    transposed(lat, lat_t)
    sum1[...] = jnp.zeros(sum1.shape, F32)
    sum2[...] = jnp.zeros(sum2.shape, F32)

    def score(c, carry):
        arrived(there, c)
        pair_patch(c, x, part, inv, ret)
        back[c, m] = ret[c, m]
        for o in ORDER:
            returned(c, o).start()
        return carry

    lax.fori_loop(0, NCHUNK, score, 0)

    def backward(c, carry):
        arrived(returned, c)
        backward_chunk(c, back, own, weight, wo_t, pre, go, gp)
        accumulate(c, hid_t, go, sum2)
        accumulate(c, lat_t, gp, sum1)
        return carry

    lax.fori_loop(0, NCHUNK - 1, backward, 0)
    arrived(returned, NCHUNK - 1)
    backward_chunk(NCHUNK - 1, back, own, weight, wo_t, pre, go, gp)

    slots = iter(range(SLOTS))
    sent = []

    def send(src, dst, device):
        at = next(slots)
        copy = pltpu.make_async_remote_copy(
            src_ref=src, dst_ref=dst, send_sem=rs_send.at[at], recv_sem=rs_recv.at[at],
            device_id=device, device_id_type=MESH,
        )
        copy.start()
        sent.append(copy)
        return copy

    def added(own_ref, landed, copies):
        for copy in copies:
            copy.wait_recv()
        total = own_ref[...]
        for ref in landed:
            total = total + ref[...]
        own_ref[...] = total

    class Group:
        def __init__(self, q, core_in, hop_in, near_in, far_in, second_in, third_in, at_p, at_q, p, q_at, z_send, z_recv):
            self.q, self.core_in, self.hop_in, self.near_in, self.far_in = q, core_in, hop_in, near_in, far_in
            self.second_in, self.third_in, self.at_p, self.at_q = second_in, third_in, at_p, at_q
            self.p, self.q_at, self.z_send, self.z_recv = p, q_at, z_send, z_recv
            self.core_copy, self.hop, self.near, self.far, self.second = {}, {}, {}, {}, {}

        def part(self, to, h, k):
            return self.q.at[core, to, pl.ds(2 * h, 2), pl.ds(2 * k, 2)]

        def exchange(self, k):
            self.core_copy[k] = send(
                self.q.at[1 - core, :, :, pl.ds(2 * k, 2)], self.core_in.at[k], at_core()
            )

        def first(self, k):
            added(self.q.at[core, :, :, pl.ds(2 * k, 2)], [self.core_in.at[k]], [self.core_copy[k]])
            for h, s in ((0, 1), (1, 3)):
                self.hop[k, h] = send(self.part((self.p + 2) % 4, h, k), self.hop_in.at[k, h], self.at_p(s))
            for h, s in ((0, 1), (1, 3)):
                back_to = 4 - s
                self.near[k, h] = send(
                    self.part((self.p + back_to) % 4, h, k), self.near_in.at[k, h], self.at_p(back_to)
                )

        def relay(self, k):
            for h, s in ((0, 1), (1, 3)):
                added(self.hop_in.at[k, h], [self.part((self.p + s) % 4, h, k)], [self.hop[k, h]])
                self.far[k, h] = send(self.hop_in.at[k, h], self.far_in.at[k, h], self.at_p(s))

        def finish(self, k):
            for h in range(2):
                added(
                    self.part(self.p, h, k), [self.near_in.at[k, h], self.far_in.at[k, h]],
                    [self.near[k, h], self.far[k, h]],
                )

        def other_ring(self, i):
            zs = pl.ds(4 * i, 4)
            self.second[i] = [
                send(self.q.at[core, self.p, (self.q_at + o) % 4, zs], self.second_in.at[i, o - 1], self.at_q(o))
                for o in (2, 1, 3)
            ]

        def collect(self, i):
            landed = [self.second_in.at[i, o] for o in range(3)]
            added(self.q.at[core, self.p, self.q_at, pl.ds(4 * i, 4)], landed, self.second[i])

        def to_z(self, o):
            return pltpu.make_async_remote_copy(
                src_ref=self.q.at[core, self.p, self.q_at, (z + o) % 8], dst_ref=self.third_in.at[o - 1],
                send_sem=self.z_send.at[o - 1], recv_sem=self.z_recv.at[o - 1],
                device_id=at_z(o), device_id_type=MESH,
            )

        def along_z(self, i):
            for j in range(4):
                o = (4 * i + j + 8 - z) % 8

                @pl.when(o != 0)
                def start():
                    self.to_z(o).start()

        def z_copies(self):
            return [self.to_z(o) for o in range(1, 8)]

        def result(self):
            return last(self.q[core, self.p, self.q_at, z], self.third_in, self.z_copies())

    def last(value, landed, copies):
        for copy in copies:
            copy.wait_recv()
        for j in range(landed.shape[0]):
            value = value + landed[j]
        return value

    ga = Group(qa, a0, ah, an, af, a2, a3, at_x, at_y, xx, y, za_send, za_recv)
    gb = Group(qb, b0, bh, bn, bf, b2, b3, at_y, at_x, y, xx, zb_send, zb_recv)
    both = (ga, gb)

    def product(k):
        g = last_chunk(lat_t, gp, sum1, k)
        for j in range(2):
            a_lo, a_hi = halves(g[j, ..., :256], g[j, ..., 256:512])
            b_lo, b_hi = halves(g[j, ..., 512:768], g[j, ..., 768:])
            for lo in range(2):
                for x_ in range(4):
                    for core_ in range(2):
                        qa[core_, x_, lo, 2 * k + j] = a_lo[lo, x_, core_]
                        qa[core_, x_, 2 + lo, 2 * k + j] = a_hi[lo, x_, core_]
                        qb[core_, lo, x_, 2 * k + j] = b_lo[lo, x_, core_]
                        qb[core_, 2 + lo, x_, 2 * k + j] = b_hi[lo, x_, core_]
        for group in both:
            group.exchange(k)

    def each(name, i):
        for group in both:
            getattr(group, name)(i)

    for k in range(4):
        g = last_chunk(hid_t, go, sum2, k)
        for j in range(2):
            c_lo, c_hi = halves(g[j, 0], g[j, 1])
            for x_ in range(4):
                for core_ in range(2):
                    qc[core_, 2 * k + j, x_, 0] = c_lo[x_, core_]
                    qc[core_, 2 * k + j, x_, 1] = c_hi[x_, core_]
    c_core = send(qc.at[1 - core], c0, at_core())
    product(0)
    product(1)
    added(qc.at[core], [c0], [c_core])
    c_one = [send(qc.at[core, (z + o) % 8], c1.at[o - 1], at_z(o)) for o in (4, 3, 5, 2, 6, 1, 7)]
    each("first", 0)
    product(2)
    each("first", 1)
    product(3)
    each("relay", 0)
    each("first", 2)
    each("relay", 1)
    each("first", 3)
    each("relay", 2)
    each("relay", 3)
    each("finish", 0)
    each("finish", 1)
    each("other_ring", 0)
    added(qc.at[core, z], [c1.at[j] for j in range(7)], c_one)
    c_two = [send(qc.at[core, z, (xx + o) % 4], c2.at[o - 1], at_x(o)) for o in (2, 1, 3)]
    each("finish", 2)
    each("finish", 3)
    each("other_ring", 1)
    added(qc.at[core, z, xx], [c2.at[j] for j in range(3)], c_two)
    c_three = [send(qc.at[core, z, xx, (y + o) % 4 // 2], c3.at[o - 1], at_y(o)) for o in (2, 1, 3)]
    each("collect", 0)
    each("along_z", 0)
    each("collect", 1)
    each("along_z", 1)
    total = last(qc[core, z, xx, b], c3, c_three)
    out[:, 512:] = jnp.where(y_lo == 0, total, pltpu.roll(total, 4, 0))
    out[:, :256] = ga.result()
    out[:, 256:512] = gb.result()

    for copy in sent + ga.z_copies() + gb.z_copies():
        copy.wait_send()

    def drained(c, carry):
        for o in range(1, MEMBERS):
            there(c, o).wait_send()
            returned(c, o).wait_send()
        return carry

    lax.fori_loop(0, NCHUNK, drained, 0)


def scratch():
    v = pltpu.VMEM
    return [
        v((ROWS, D), BF16), v((D, HID), BF16), v((CH, HID), BF16), v((HID, LANE), BF16), v((LANE, HID), BF16),
        v((POOL, FEAT), BF16), v((1, NPATCH), jnp.int32), v((1, NPATCH), jnp.int32),
        v((ROWS, HID), F32), v((ROWS, HID), BF16), v((NCHUNK, MEMBERS, PATCH, LANE), F32), v((NCHUNK, MEMBERS, PATCH, LANE), F32),
        v((MEMBERS, NCHUNK, PATCH, LANE), F32), v((NPATCH, FEAT), BF16), v((ROWS, LANE), F32),
        v((ROWS, LANE), F32), v((ROWS, LANE), F32), v((len(PAIRS), 8, LANE), F32), v((len(PAIRS), LANE), F32),
        v((NCHUNK, MEMBERS, PATCH, LANE), F32), v((NCHUNK, MEMBERS, PATCH, LANE), F32),
        v((ROWS, LANE), BF16), v((ROWS, HID), BF16), v((D, ROWS), BF16), v((HID, ROWS), BF16),
        v((D, HID), F32), v((HID, LANE), F32),
        v((2, 4, 4, 8, 8, 256), F32), v((2, 4, 4, 8, 8, 256), F32), v((2, 8, 4, 2, 8, 128), F32),
        v((4, 4, 4, 2, 8, 256), F32), v((4, 4, 4, 2, 8, 256), F32), v((8, 4, 2, 8, 128), F32),
        v((4, 2, 2, 2, 8, 256), F32), v((4, 2, 2, 2, 8, 256), F32), v((7, 4, 2, 8, 128), F32),
        v((4, 2, 2, 2, 8, 256), F32), v((4, 2, 2, 2, 8, 256), F32),
        v((4, 2, 2, 2, 8, 256), F32), v((4, 2, 2, 2, 8, 256), F32),
        v((2, 3, 4, 8, 256), F32), v((2, 3, 4, 8, 256), F32), v((3, 2, 8, 128), F32),
        v((7, 8, 256), F32), v((7, 8, 256), F32), v((3, 8, 128), F32),
        pltpu.SemaphoreType.DMA((9,)),
        pltpu.SemaphoreType.DMA((NCHUNK, MEMBERS)), pltpu.SemaphoreType.DMA((NCHUNK, MEMBERS)),
        pltpu.SemaphoreType.DMA((NCHUNK, MEMBERS)), pltpu.SemaphoreType.DMA((NCHUNK, MEMBERS)),
        pltpu.SemaphoreType.DMA((SLOTS,)), pltpu.SemaphoreType.DMA((SLOTS,)),
        pltpu.SemaphoreType.DMA((7,)), pltpu.SemaphoreType.DMA((7,)),
        pltpu.SemaphoreType.DMA((7,)), pltpu.SemaphoreType.DMA((7,)),
    ]


def unpack(packed, out1, out2):
    for i in range(2):
        value = packed[:, i * 256 : i * 256 + 256]
        out1[:, i * 512 : i * 512 + 256] = value[:4]
        out1[:, i * 512 + 256 : i * 512 + 512] = pltpu.roll(value, 4, 0)[:4]
    out2[...] = packed[:4, 512 : 512 + CH]


def shards(latent, w_in, w_out, observed, patch_index, counts):
    packed = pl.pallas_call(
        kernel,
        out_shape=jax.ShapeDtypeStruct((8, 640), F32),
        in_specs=[pl.BlockSpec(memory_space=pl.ANY)] * 6,
        out_specs=pl.BlockSpec(memory_space=pltpu.VMEM),
        scratch_shapes=scratch(),
        compiler_params=pltpu.CompilerParams(
            collective_id=0, has_side_effects=True, vmem_limit_bytes=VMEM_KIB * 1024
        ),
    )(latent, w_in, w_out.T, observed, patch_index, counts)
    return pl.pallas_call(
        unpack,
        out_shape=(jax.ShapeDtypeStruct((4, HID), F32), jax.ShapeDtypeStruct((4, CH), F32)),
        compiler_params=pltpu.CompilerParams(vmem_limit_bytes=1024 * 1024),
    )(packed)


def solution(mesh):
    placed = (
        P("member", "batch", "tile", None),
        P(),
        P(),
        P("batch", "tile", None),
        P("batch", "tile"),
        P("batch", "tile"),
    )
    rows = P(("member", "tile", "batch"), None)
    return jax.shard_map(
        shards, mesh=mesh, in_specs=placed, out_specs=(rows, rows), check_vma=False
    )
```

```python
import jax
import jax.numpy as jnp
from jax import lax
from jax.experimental import pallas as pl
from jax.experimental.pallas import tpu as pltpu
from jax.sharding import PartitionSpec as P

MESH = pl.DeviceIdType.MESH
F32, BF16 = jnp.float32, jnp.bfloat16
ROWS, D, HID, CH, LANE = 1024, 1024, 1024, 112, 128
PATCH, NPATCH, MEMBERS, POOL, FEAT = 16, 64, 16, 128, 1792
NCHUNK, CROWS = 4, 256
SLOTS = 82
VMEM_KIB = 55100
SENT = 14
ORDER = (8, 7, 9, 6, 10, 5, 11, 4, 12, 3, 13, 2, 14, 1, 15)
PAIRS = [(i, k) for i in range(MEMBERS) for k in range(i + 1, MEMBERS)]
PAIR_AT = {pair: at for at, pair in enumerate(PAIRS)}


def row_and_lane(shape):
    return lax.broadcasted_iota(jnp.int32, shape, 0), lax.broadcasted_iota(jnp.int32, shape, 1)


def pack_patch(value):
    row, lane = row_and_lane((PATCH, LANE))
    low = jnp.broadcast_to(value[14:15], (PATCH, LANE))
    high = pltpu.roll(jnp.broadcast_to(value[15:16], (PATCH, LANE)), 16, 1)
    moved = pltpu.roll(jnp.where(row < 7, low, high), 16, 1, stride=16, stride_axis=0)
    return jnp.where(row < SENT, jnp.where(lane < CH, value, moved), 0.0)


def unpack_patch(value):
    row, lane = row_and_lane((PATCH, LANE))
    moved = jnp.where((lane >= CH) & (row < SENT), value, 0.0)
    groups = jnp.where(row < 7, 7 - row, 14 - row)
    for bit in (4, 2, 1):
        moved = jnp.where((groups & bit) != 0, pltpu.roll(moved, 16 * bit, 1), moved)
    low = jnp.sum(jnp.where(row < 7, moved, 0.0), axis=0, keepdims=True)
    high = jnp.sum(jnp.where(row < 7, 0.0, moved), axis=0, keepdims=True)
    tail = jnp.where(row == 14, low, high)
    return jnp.where(row < SENT, jnp.where(lane < CH, value, 0.0), tail)


def forward_chunk(c, lat, w_in, wo, pre, hid, dec, packed):
    rows = pl.ds(pl.multiple_of(c * CROWS, CROWS), CROWS)
    v = jnp.dot(lat[rows, :], w_in[...], preferred_element_type=F32)
    pre[rows, :] = v
    hid[rows, :] = (v * (1.0 / (1.0 + jnp.exp(-v)))).astype(BF16)
    out = jnp.dot(hid[rows, :], wo[...], preferred_element_type=F32)
    dec[c] = out.reshape(MEMBERS, PATCH, LANE)
    for j in range(MEMBERS):
        packed[c, j] = pack_patch(out[j * PATCH : j * PATCH + PATCH])


def slopes(pre):
    def step(i, carry):
        rows = pl.ds(pl.multiple_of(i * 64, 64), 64)
        v = pre[rows, :]
        sigma = 1.0 / (1.0 + jnp.exp(-v))
        pre[rows, :] = sigma * (1.0 + v * (1.0 - sigma))
        return carry

    lax.fori_loop(0, ROWS // 64, step, 0)


def transposed(src, dst):
    def step(i, carry):
        at = pl.ds(pl.multiple_of(i * 128, 128), 128)
        dst[at, :] = src[:, at].T
        return carry

    lax.fori_loop(0, 8, step, 0)


def own_term(obs, idx, cnt, dec, tgt, target, own, weight):
    pool_at = lax.broadcasted_iota(jnp.int32, (POOL, NPATCH), 0)
    choose = (pool_at == idx[...]).astype(F32).astype(BF16)
    picked = lax.dot_general(choose, obs[...], (((0,), (0,)), ((), ())), preferred_element_type=F32)
    tgt[...] = picked.astype(BF16)
    entry = lax.broadcasted_iota(jnp.int32, (256, LANE), 0)
    lane = lax.broadcasted_iota(jnp.int32, (256, LANE), 1)
    for i in range(PATCH):
        start = min(CH * i // 128 * 128, FEAT - 256)
        shift = ((entry == lane + (CH * i - start)) & (lane < CH)).astype(F32).astype(BF16)
        one = jnp.dot(tgt[:, start : start + 256], shift, preferred_element_type=F32)
        target[pl.ds(i, NPATCH, stride=PATCH), :] = one
    counts = cnt[...].astype(F32)

    def step(c, carry):
        rows = pl.ds(pl.multiple_of(c * CROWS, CROWS), CROWS)
        patch_of = (lax.broadcasted_iota(jnp.int32, (CROWS, NPATCH), 0) + c * CROWS) // PATCH
        at = lax.broadcasted_iota(jnp.int32, (CROWS, NPATCH), 1)
        count = jnp.sum(jnp.where(patch_of == at, counts, 0.0), axis=1, keepdims=True)
        delta = dec[c].reshape(CROWS, LANE) - target[rows, :]
        square = jnp.sum((delta * delta).reshape(MEMBERS, PATCH, LANE), axis=(1, 2), keepdims=True)
        scale = (1.0 / (MEMBERS * jnp.sqrt(square + 1.0))) * jnp.ones((MEMBERS, PATCH, LANE), F32)
        own[rows, :] = delta * scale.reshape(CROWS, LANE) * count
        weight[rows, :] = jnp.broadcast_to(count * (1.0 / (MEMBERS * MEMBERS)), (CROWS, LANE))
        return carry

    lax.fori_loop(0, NCHUNK, step, 0)


def pair_patch(c, x, part, inv, out):
    xs = [x[k, c] for k in range(MEMBERS)]
    for at, (i, k) in enumerate(PAIRS):
        d = xs[i] - xs[k]
        d = d * d
        part[at] = d[:8] + d[8:]
    total = jnp.sum(jnp.sum(part[...], axis=1), axis=1, keepdims=True)
    inv[...] = jnp.broadcast_to(1.0 / jnp.sqrt(total + 1.0), inv.shape)
    for i in range(MEMBERS):
        acc = None
        for k in range(MEMBERS):
            if k == i:
                continue
            at = PAIR_AT[(min(i, k), max(i, k))]
            term = (xs[i] - xs[k]) * inv[at : at + 1, :]
            acc = term if acc is None else acc + term
        out[c, i] = acc


def grad_chunk(c, back, own, weight, go):
    rows = pl.ds(pl.multiple_of(c * CROWS, CROWS), CROWS)
    pair = jnp.concatenate([unpack_patch(back[c, j]) for j in range(MEMBERS)], axis=0)
    grad = (own[rows, :] - weight[rows, :] * pair).astype(BF16)
    go[rows, :] = grad


def slope_chunk(c, wo_t, slope, go, gp):
    rows = pl.ds(pl.multiple_of(c * CROWS, CROWS), CROWS)
    gh = jnp.dot(go[rows, :], wo_t[...], preferred_element_type=F32)
    gp[rows, :] = (gh * slope[rows, :]).astype(BF16)


def accumulate(c, left, right, total):
    rows = pl.ds(pl.multiple_of(c * CROWS, CROWS), CROWS)

    def step(i, carry):
        at = pl.ds(pl.multiple_of(i * 256, 256), 256)
        total[at, :] += jnp.dot(left[at, rows], right[rows, :], preferred_element_type=F32)
        return carry

    lax.fori_loop(0, 4, step, 0)


def halves(lo, hi):
    top = lax.broadcasted_iota(jnp.int32, lo.shape, lo.ndim - 2) < 4
    axis = lo.ndim - 2
    return jnp.where(top, lo, pltpu.roll(hi, 4, axis)), jnp.where(top, pltpu.roll(lo, 4, axis), hi)


def last_chunk(left, right, total, i):
    rows = slice((NCHUNK - 1) * CROWS, NCHUNK * CROWS)
    at = slice(i * 256, i * 256 + 256)
    g = total[at, :] + jnp.dot(left[at, rows], right[rows, :], preferred_element_type=F32)
    return g.reshape(2, 2, 4, 2, 8, g.shape[1])


def kernel(
    lat_hbm, w_in_hbm, w_out_hbm, obs_hbm, idx_hbm, cnt_hbm, out,
    lat, w_in, w_raw, wo, wo_t, obs, idx, cnt, pre, hid, dec, packed, x, tgt, target, own, weight, part, inv, ret, back,
    go, gp, lat_t, hid_t, sum1, sum2, qa, qb, qc,
    a0, b0, c0, ah, bh, c1, an, bn, af, bf, a2, b2, c2, a3, b3, c3,
    load_sem, there_send, there_recv, back_send, back_recv, rs_send, rs_recv, za_send, za_recv, zb_send, zb_recv,
):
    m, t, b = lax.axis_index("member"), lax.axis_index("tile"), lax.axis_index("batch")
    z, y_lo, xx, core = m // 2, m % 2, t // 2, t % 2
    y = b * 2 + y_lo

    def at_x(o):
        return {"tile": (xx + o) % 4 * 2 + core}

    def at_y(o):
        to = (y + o) % 4
        return {"member": z * 2 + to % 2, "batch": to // 2}

    def at_z(o):
        return {"member": (z + o) % 8 * 2 + y_lo}

    def at_member(o):
        return {"member": (m + o) % MEMBERS}

    def at_core():
        return {"tile": xx * 2 + (1 - core)}

    peers = [at_member(o) for o in ORDER] + [at_core()] + [at_x(o) for o in range(1, 4)]

    def load_lat(c):
        rows = pl.ds(pl.multiple_of(c * CROWS, CROWS), CROWS)
        return pltpu.make_async_copy(lat_hbm.at[0, 0, rows, :], lat.at[rows, :], load_sem.at[c])

    load_w = pltpu.make_async_copy(w_in_hbm, w_in, load_sem.at[4])
    load_wo = pltpu.make_async_copy(w_out_hbm, w_raw, load_sem.at[5])
    later = [
        pltpu.make_async_copy(obs_hbm.at[0], obs, load_sem.at[6]),
        pltpu.make_async_copy(idx_hbm, idx, load_sem.at[7]),
        pltpu.make_async_copy(cnt_hbm, cnt, load_sem.at[8]),
    ]
    load_wo.start()
    load_w.start()
    load_lat(0).start()
    x[...] = jnp.zeros(x.shape, F32)
    barrier = pltpu.get_barrier_semaphore()
    for peer in peers:
        pl.semaphore_signal(barrier, inc=1, device_id=peer, device_id_type=MESH)
    for o in (1, 2, 3):
        pl.semaphore_signal(barrier, inc=1, device_id=at_y(o), device_id_type=MESH)
    wo_t[CH:, :] = jnp.zeros((LANE - CH, HID), BF16)
    load_wo.wait()
    wo_t[:CH, :] = w_raw[...]
    wo[...] = wo_t[...].T
    load_w.wait()
    load_lat(0).wait()
    for c in range(1, NCHUNK):
        load_lat(c).start()
    for load in later:
        load.start()

    def there(c, o):
        return pltpu.make_async_remote_copy(
            src_ref=packed.at[c, (m + o) % MEMBERS, pl.ds(0, SENT)], dst_ref=x.at[m, c, pl.ds(0, SENT)],
            send_sem=there_send.at[c, o], recv_sem=there_recv.at[c, o],
            device_id=at_member(o), device_id_type=MESH,
        )

    def returned(c, o):
        return pltpu.make_async_remote_copy(
            src_ref=ret.at[c, (m + o) % MEMBERS, pl.ds(0, SENT)], dst_ref=back.at[c, m, pl.ds(0, SENT)],
            send_sem=back_send.at[c, o], recv_sem=back_recv.at[c, o],
            device_id=at_member(o), device_id_type=MESH,
        )

    def arrived(make, c):
        for o in range(1, MEMBERS):
            make(c, o).wait_recv()

    def forward(c, carry):
        forward_chunk(c, lat, w_in, wo, pre, hid, dec, packed)
        return carry

    def depart(c):
        x[m, c] = packed[c, m]
        for o in ORDER:
            there(c, o).start()

    def forward_and_depart(c, carry):
        load_lat(c).wait()
        forward(c, carry)
        depart(c)
        return carry

    forward(0, 0)
    pl.semaphore_wait(barrier, len(peers) + 3)
    depart(0)
    lax.fori_loop(1, NCHUNK, forward_and_depart, 0)

    for load in later:
        load.wait()
    own_term(obs, idx, cnt, dec, tgt, target, own, weight)
    slopes(pre)
    transposed(hid, hid_t)
    transposed(lat, lat_t)
    sum1[...] = jnp.zeros(sum1.shape, F32)
    sum2[...] = jnp.zeros(sum2.shape, F32)

    def score(c, carry):
        arrived(there, c)
        pair_patch(c, x, part, inv, ret)
        back[c, m] = ret[c, m]
        for o in ORDER:
            returned(c, o).start()
        return carry

    lax.fori_loop(0, NCHUNK, score, 0)

    def backward(c, carry):
        arrived(returned, c)
        grad_chunk(c, back, own, weight, go)
        slope_chunk(c, wo_t, pre, go, gp)
        accumulate(c, hid_t, go, sum2)
        accumulate(c, lat_t, gp, sum1)
        return carry

    lax.fori_loop(0, NCHUNK - 1, backward, 0)
    arrived(returned, NCHUNK - 1)
    grad_chunk(NCHUNK - 1, back, own, weight, go)

    slots = iter(range(SLOTS))
    sent = []

    def send(src, dst, device):
        at = next(slots)
        copy = pltpu.make_async_remote_copy(
            src_ref=src, dst_ref=dst, send_sem=rs_send.at[at], recv_sem=rs_recv.at[at],
            device_id=device, device_id_type=MESH,
        )
        copy.start()
        sent.append(copy)
        return copy

    def added(own_ref, landed, copies):
        for copy in copies:
            copy.wait_recv()
        total = own_ref[...]
        for ref in landed:
            total = total + ref[...]
        own_ref[...] = total

    class Group:
        def __init__(self, q, core_in, hop_in, near_in, far_in, second_in, third_in, at_p, at_q, p, q_at, z_send, z_recv):
            self.q, self.core_in, self.hop_in, self.near_in, self.far_in = q, core_in, hop_in, near_in, far_in
            self.second_in, self.third_in, self.at_p, self.at_q = second_in, third_in, at_p, at_q
            self.p, self.q_at, self.z_send, self.z_recv = p, q_at, z_send, z_recv
            self.core_copy, self.hop, self.near, self.far, self.second = {}, {}, {}, {}, {}

        def part(self, to, h, k):
            return self.q.at[core, to, pl.ds(2 * h, 2), pl.ds(2 * k, 2)]

        def exchange(self, k):
            self.core_copy[k] = send(
                self.q.at[1 - core, :, :, pl.ds(2 * k, 2)], self.core_in.at[k], at_core()
            )

        def first(self, k):
            added(self.q.at[core, :, :, pl.ds(2 * k, 2)], [self.core_in.at[k]], [self.core_copy[k]])
            for h, s in ((0, 1), (1, 3)):
                self.hop[k, h] = send(self.part((self.p + 2) % 4, h, k), self.hop_in.at[k, h], self.at_p(s))
            for h, s in ((0, 1), (1, 3)):
                back_to = 4 - s
                self.near[k, h] = send(
                    self.part((self.p + back_to) % 4, h, k), self.near_in.at[k, h], self.at_p(back_to)
                )

        def relay(self, k):
            for h, s in ((0, 1), (1, 3)):
                added(self.hop_in.at[k, h], [self.part((self.p + s) % 4, h, k)], [self.hop[k, h]])
                self.far[k, h] = send(self.hop_in.at[k, h], self.far_in.at[k, h], self.at_p(s))

        def finish(self, k):
            for h in range(2):
                added(
                    self.part(self.p, h, k), [self.near_in.at[k, h], self.far_in.at[k, h]],
                    [self.near[k, h], self.far[k, h]],
                )

        def other_ring(self, i):
            zs = pl.ds(4 * i, 4)
            self.second[i] = [
                send(self.q.at[core, self.p, (self.q_at + o) % 4, zs], self.second_in.at[i, o - 1], self.at_q(o))
                for o in (2, 1, 3)
            ]

        def collect(self, i):
            landed = [self.second_in.at[i, o] for o in range(3)]
            added(self.q.at[core, self.p, self.q_at, pl.ds(4 * i, 4)], landed, self.second[i])

        def to_z(self, o):
            return pltpu.make_async_remote_copy(
                src_ref=self.q.at[core, self.p, self.q_at, (z + o) % 8], dst_ref=self.third_in.at[o - 1],
                send_sem=self.z_send.at[o - 1], recv_sem=self.z_recv.at[o - 1],
                device_id=at_z(o), device_id_type=MESH,
            )

        def along_z(self, i):
            for j in range(4):
                o = (4 * i + j + 8 - z) % 8

                @pl.when(o != 0)
                def start():
                    self.to_z(o).start()

        def z_copies(self):
            return [self.to_z(o) for o in range(1, 8)]

        def result(self):
            return last(self.q[core, self.p, self.q_at, z], self.third_in, self.z_copies())

    def last(value, landed, copies):
        for copy in copies:
            copy.wait_recv()
        for j in range(landed.shape[0]):
            value = value + landed[j]
        return value

    ga = Group(qa, a0, ah, an, af, a2, a3, at_x, at_y, xx, y, za_send, za_recv)
    gb = Group(qb, b0, bh, bn, bf, b2, b3, at_y, at_x, y, xx, zb_send, zb_recv)
    both = (ga, gb)

    def product(k):
        g = last_chunk(lat_t, gp, sum1, k)
        for j in range(2):
            a_lo, a_hi = halves(g[j, ..., :256], g[j, ..., 256:512])
            b_lo, b_hi = halves(g[j, ..., 512:768], g[j, ..., 768:])
            for lo in range(2):
                for x_ in range(4):
                    for core_ in range(2):
                        qa[core_, x_, lo, 2 * k + j] = a_lo[lo, x_, core_]
                        qa[core_, x_, 2 + lo, 2 * k + j] = a_hi[lo, x_, core_]
                        qb[core_, lo, x_, 2 * k + j] = b_lo[lo, x_, core_]
                        qb[core_, 2 + lo, x_, 2 * k + j] = b_hi[lo, x_, core_]
        for group in both:
            group.exchange(k)

    def each(name, i):
        for group in both:
            getattr(group, name)(i)

    for k in range(4):
        g = last_chunk(hid_t, go, sum2, k)
        for j in range(2):
            c_lo, c_hi = halves(g[j, 0], g[j, 1])
            for x_ in range(4):
                for core_ in range(2):
                    qc[core_, 2 * k + j, x_, 0] = c_lo[x_, core_]
                    qc[core_, 2 * k + j, x_, 1] = c_hi[x_, core_]
    c_core = send(qc.at[1 - core], c0, at_core())
    slope_chunk(NCHUNK - 1, wo_t, pre, go, gp)
    product(0)
    product(1)
    added(qc.at[core], [c0], [c_core])
    c_one = [send(qc.at[core, (z + o) % 8], c1.at[o - 1], at_z(o)) for o in (4, 3, 5, 2, 6, 1, 7)]
    each("first", 0)
    product(2)
    each("first", 1)
    product(3)
    each("relay", 0)
    each("first", 2)
    each("relay", 1)
    each("first", 3)
    each("relay", 2)
    each("relay", 3)
    each("finish", 0)
    each("finish", 1)
    each("other_ring", 0)
    added(qc.at[core, z], [c1.at[j] for j in range(7)], c_one)
    c_two = [send(qc.at[core, z, (xx + o) % 4], c2.at[o - 1], at_x(o)) for o in (2, 1, 3)]
    each("finish", 2)
    each("finish", 3)
    each("other_ring", 1)
    added(qc.at[core, z, xx], [c2.at[j] for j in range(3)], c_two)
    c_three = [send(qc.at[core, z, xx, (y + o) % 4 // 2], c3.at[o - 1], at_y(o)) for o in (2, 1, 3)]
    each("collect", 0)
    each("along_z", 0)
    each("collect", 1)
    each("along_z", 1)
    total = last(qc[core, z, xx, b], c3, c_three)
    out[:, 512:] = jnp.where(y_lo == 0, total, pltpu.roll(total, 4, 0))
    out[:, :256] = ga.result()
    out[:, 256:512] = gb.result()

    for copy in sent + ga.z_copies() + gb.z_copies():
        copy.wait_send()

    def drained(c, carry):
        for o in range(1, MEMBERS):
            there(c, o).wait_send()
            returned(c, o).wait_send()
        return carry

    lax.fori_loop(0, NCHUNK, drained, 0)


def scratch():
    v = pltpu.VMEM
    return [
        v((ROWS, D), BF16), v((D, HID), BF16), v((CH, HID), BF16), v((HID, LANE), BF16), v((LANE, HID), BF16),
        v((POOL, FEAT), BF16), v((1, NPATCH), jnp.int32), v((1, NPATCH), jnp.int32),
        v((ROWS, HID), F32), v((ROWS, HID), BF16), v((NCHUNK, MEMBERS, PATCH, LANE), F32), v((NCHUNK, MEMBERS, PATCH, LANE), F32),
        v((MEMBERS, NCHUNK, PATCH, LANE), F32), v((NPATCH, FEAT), BF16), v((ROWS, LANE), F32),
        v((ROWS, LANE), F32), v((ROWS, LANE), F32), v((len(PAIRS), 8, LANE), F32), v((len(PAIRS), LANE), F32),
        v((NCHUNK, MEMBERS, PATCH, LANE), F32), v((NCHUNK, MEMBERS, PATCH, LANE), F32),
        v((ROWS, LANE), BF16), v((ROWS, HID), BF16), v((D, ROWS), BF16), v((HID, ROWS), BF16),
        v((D, HID), F32), v((HID, LANE), F32),
        v((2, 4, 4, 8, 8, 256), F32), v((2, 4, 4, 8, 8, 256), F32), v((2, 8, 4, 2, 8, 128), F32),
        v((4, 4, 4, 2, 8, 256), F32), v((4, 4, 4, 2, 8, 256), F32), v((8, 4, 2, 8, 128), F32),
        v((4, 2, 2, 2, 8, 256), F32), v((4, 2, 2, 2, 8, 256), F32), v((7, 4, 2, 8, 128), F32),
        v((4, 2, 2, 2, 8, 256), F32), v((4, 2, 2, 2, 8, 256), F32),
        v((4, 2, 2, 2, 8, 256), F32), v((4, 2, 2, 2, 8, 256), F32),
        v((2, 3, 4, 8, 256), F32), v((2, 3, 4, 8, 256), F32), v((3, 2, 8, 128), F32),
        v((7, 8, 256), F32), v((7, 8, 256), F32), v((3, 8, 128), F32),
        pltpu.SemaphoreType.DMA((9,)),
        pltpu.SemaphoreType.DMA((NCHUNK, MEMBERS)), pltpu.SemaphoreType.DMA((NCHUNK, MEMBERS)),
        pltpu.SemaphoreType.DMA((NCHUNK, MEMBERS)), pltpu.SemaphoreType.DMA((NCHUNK, MEMBERS)),
        pltpu.SemaphoreType.DMA((SLOTS,)), pltpu.SemaphoreType.DMA((SLOTS,)),
        pltpu.SemaphoreType.DMA((7,)), pltpu.SemaphoreType.DMA((7,)),
        pltpu.SemaphoreType.DMA((7,)), pltpu.SemaphoreType.DMA((7,)),
    ]


def unpack(packed, out1, out2):
    for i in range(2):
        value = packed[:, i * 256 : i * 256 + 256]
        out1[:, i * 512 : i * 512 + 256] = value[:4]
        out1[:, i * 512 + 256 : i * 512 + 512] = pltpu.roll(value, 4, 0)[:4]
    out2[...] = packed[:4, 512 : 512 + CH]


def shards(latent, w_in, w_out, observed, patch_index, counts):
    packed = pl.pallas_call(
        kernel,
        out_shape=jax.ShapeDtypeStruct((8, 640), F32),
        in_specs=[pl.BlockSpec(memory_space=pl.ANY)] * 6,
        out_specs=pl.BlockSpec(memory_space=pltpu.VMEM),
        scratch_shapes=scratch(),
        compiler_params=pltpu.CompilerParams(
            collective_id=0, has_side_effects=True, vmem_limit_bytes=VMEM_KIB * 1024
        ),
    )(latent, w_in, w_out.T, observed, patch_index, counts)
    return pl.pallas_call(
        unpack,
        out_shape=(jax.ShapeDtypeStruct((4, HID), F32), jax.ShapeDtypeStruct((4, CH), F32)),
        compiler_params=pltpu.CompilerParams(vmem_limit_bytes=1024 * 1024),
    )(packed)


def solution(mesh):
    placed = (
        P("member", "batch", "tile", None),
        P(),
        P(),
        P("batch", "tile", None),
        P("batch", "tile"),
        P("batch", "tile"),
    )
    rows = P(("member", "tile", "batch"), None)
    return jax.shard_map(
        shards, mesh=mesh, in_specs=placed, out_specs=(rows, rows), check_vma=False
    )
```

```python
import jax
import jax.numpy as jnp
from jax import lax
from jax.experimental import pallas as pl
from jax.experimental.pallas import tpu as pltpu
from jax.sharding import PartitionSpec as P

MESH = pl.DeviceIdType.MESH
F32, BF16 = jnp.float32, jnp.bfloat16
ROWS, D, HID, CH, LANE = 1024, 1024, 1024, 112, 128
PATCH, NPATCH, MEMBERS, POOL, FEAT = 16, 64, 16, 128, 1792
NCHUNK, CROWS = 4, 256
SLOTS = 82
VMEM_KIB = 55100
SENT = 14
ORDER = (8, 7, 9, 6, 10, 5, 11, 4, 12, 3, 13, 2, 14, 1, 15)
PAIRS = [(i, k) for i in range(MEMBERS) for k in range(i + 1, MEMBERS)]
PAIR_AT = {pair: at for at, pair in enumerate(PAIRS)}


def row_and_lane(shape):
    return lax.broadcasted_iota(jnp.int32, shape, 0), lax.broadcasted_iota(jnp.int32, shape, 1)


def pack_patch(value):
    row, lane = row_and_lane((PATCH, LANE))
    low = jnp.broadcast_to(value[14:15], (PATCH, LANE))
    high = pltpu.roll(jnp.broadcast_to(value[15:16], (PATCH, LANE)), 16, 1)
    moved = pltpu.roll(jnp.where(row < 7, low, high), 16, 1, stride=16, stride_axis=0)
    return jnp.where(row < SENT, jnp.where(lane < CH, value, moved), 0.0)


def unpack_patch(value):
    row, lane = row_and_lane((PATCH, LANE))
    moved = jnp.where((lane >= CH) & (row < SENT), value, 0.0)
    groups = jnp.where(row < 7, 7 - row, 14 - row)
    for bit in (4, 2, 1):
        moved = jnp.where((groups & bit) != 0, pltpu.roll(moved, 16 * bit, 1), moved)
    low = jnp.sum(jnp.where(row < 7, moved, 0.0), axis=0, keepdims=True)
    high = jnp.sum(jnp.where(row < 7, 0.0, moved), axis=0, keepdims=True)
    tail = jnp.where(row == 14, low, high)
    return jnp.where(row < SENT, jnp.where(lane < CH, value, 0.0), tail)


def forward_chunk(c, lat, w_in, wo, pre, hid, dec, packed):
    rows = pl.ds(pl.multiple_of(c * CROWS, CROWS), CROWS)
    v = jnp.dot(lat[rows, :], w_in[...], preferred_element_type=F32)
    pre[rows, :] = v
    hid[rows, :] = (v * (1.0 / (1.0 + jnp.exp(-v)))).astype(BF16)
    out = jnp.dot(hid[rows, :], wo[...], preferred_element_type=F32)
    dec[c] = out.reshape(MEMBERS, PATCH, LANE)
    for j in range(MEMBERS):
        packed[c, j] = pack_patch(out[j * PATCH : j * PATCH + PATCH])


def slopes(pre):
    def step(i, carry):
        rows = pl.ds(pl.multiple_of(i * 64, 64), 64)
        v = pre[rows, :]
        sigma = 1.0 / (1.0 + jnp.exp(-v))
        pre[rows, :] = sigma * (1.0 + v * (1.0 - sigma))
        return carry

    lax.fori_loop(0, ROWS // 64, step, 0)


def transposed(src, dst):
    def step(i, carry):
        at = pl.ds(pl.multiple_of(i * 128, 128), 128)
        dst[at, :] = src[:, at].T
        return carry

    lax.fori_loop(0, 8, step, 0)


def own_term(obs, idx, cnt, dec, tgt, target, own, weight):
    pool_at = lax.broadcasted_iota(jnp.int32, (POOL, NPATCH), 0)
    choose = (pool_at == idx[...]).astype(F32).astype(BF16)
    picked = lax.dot_general(choose, obs[...], (((0,), (0,)), ((), ())), preferred_element_type=F32)
    tgt[...] = picked.astype(BF16)
    entry = lax.broadcasted_iota(jnp.int32, (256, LANE), 0)
    lane = lax.broadcasted_iota(jnp.int32, (256, LANE), 1)
    for i in range(PATCH):
        start = min(CH * i // 128 * 128, FEAT - 256)
        shift = ((entry == lane + (CH * i - start)) & (lane < CH)).astype(F32).astype(BF16)
        one = jnp.dot(tgt[:, start : start + 256], shift, preferred_element_type=F32)
        target[pl.ds(i, NPATCH, stride=PATCH), :] = one
    counts = cnt[...].astype(F32)

    def step(c, carry):
        rows = pl.ds(pl.multiple_of(c * CROWS, CROWS), CROWS)
        patch_of = (lax.broadcasted_iota(jnp.int32, (CROWS, NPATCH), 0) + c * CROWS) // PATCH
        at = lax.broadcasted_iota(jnp.int32, (CROWS, NPATCH), 1)
        count = jnp.sum(jnp.where(patch_of == at, counts, 0.0), axis=1, keepdims=True)
        delta = dec[c].reshape(CROWS, LANE) - target[rows, :]
        square = jnp.sum((delta * delta).reshape(MEMBERS, PATCH, LANE), axis=(1, 2), keepdims=True)
        scale = (1.0 / (MEMBERS * jnp.sqrt(square + 1.0))) * jnp.ones((MEMBERS, PATCH, LANE), F32)
        own[rows, :] = delta * scale.reshape(CROWS, LANE) * count
        weight[rows, :] = jnp.broadcast_to(count * (1.0 / (MEMBERS * MEMBERS)), (CROWS, LANE))
        return carry

    lax.fori_loop(0, NCHUNK, step, 0)


def pair_patch(c, x, part, inv, out):
    xs = [x[k, c] for k in range(MEMBERS)]
    for at, (i, k) in enumerate(PAIRS):
        d = xs[i] - xs[k]
        d = d * d
        part[at] = d[:8] + d[8:]
    total = jnp.sum(jnp.sum(part[...], axis=1), axis=1, keepdims=True)
    inv[...] = jnp.broadcast_to(1.0 / jnp.sqrt(total + 1.0), inv.shape)
    for i in range(MEMBERS):
        acc = None
        for k in range(MEMBERS):
            if k == i:
                continue
            at = PAIR_AT[(min(i, k), max(i, k))]
            term = (xs[i] - xs[k]) * inv[at : at + 1, :]
            acc = term if acc is None else acc + term
        out[c, i] = acc


def grad_chunk(c, back, own, weight, go):
    rows = pl.ds(pl.multiple_of(c * CROWS, CROWS), CROWS)
    pair = jnp.concatenate([unpack_patch(back[c, j]) for j in range(MEMBERS)], axis=0)
    grad = (own[rows, :] - weight[rows, :] * pair).astype(BF16)
    go[rows, :] = grad


def slope_chunk(c, wo_t, slope, go, gp):
    rows = pl.ds(pl.multiple_of(c * CROWS, CROWS), CROWS)
    gh = jnp.dot(go[rows, :], wo_t[...], preferred_element_type=F32)
    gp[rows, :] = (gh * slope[rows, :]).astype(BF16)


def accumulate(c, left, right, total):
    rows = pl.ds(pl.multiple_of(c * CROWS, CROWS), CROWS)

    def step(i, carry):
        at = pl.ds(pl.multiple_of(i * 256, 256), 256)
        total[at, :] += jnp.dot(left[at, rows], right[rows, :], preferred_element_type=F32)
        return carry

    lax.fori_loop(0, 4, step, 0)


def halves(lo, hi):
    top = lax.broadcasted_iota(jnp.int32, lo.shape, lo.ndim - 2) < 4
    axis = lo.ndim - 2
    return jnp.where(top, lo, pltpu.roll(hi, 4, axis)), jnp.where(top, pltpu.roll(lo, 4, axis), hi)


def last_chunk(left, right, total, i):
    rows = slice((NCHUNK - 1) * CROWS, NCHUNK * CROWS)
    at = slice(i * 256, i * 256 + 256)
    g = total[at, :] + jnp.dot(left[at, rows], right[rows, :], preferred_element_type=F32)
    return g.reshape(2, 2, 4, 2, 8, g.shape[1])


def kernel(
    lat_hbm, w_in_hbm, w_out_hbm, obs_hbm, idx_hbm, cnt_hbm, out,
    lat, w_in, w_raw, wo, wo_t, obs, idx, cnt, pre, hid, dec, packed, x, tgt, target, own, weight, part, inv, ret, back,
    go, gp, lat_t, hid_t, sum1, sum2, qa, qb, qc,
    a0, b0, c0, ah, bh, c1, an, bn, af, bf, a2, b2, c2, a3, b3, c3,
    load_sem, there_send, there_recv, back_send, back_recv, rs_send, rs_recv, za_send, za_recv, zb_send, zb_recv,
):
    m, t, b = lax.axis_index("member"), lax.axis_index("tile"), lax.axis_index("batch")
    z, y_lo, xx, core = m // 2, m % 2, t // 2, t % 2
    y = b * 2 + y_lo

    def at_x(o):
        return {"tile": (xx + o) % 4 * 2 + core}

    def at_y(o):
        to = (y + o) % 4
        return {"member": z * 2 + to % 2, "batch": to // 2}

    def at_z(o):
        return {"member": (z + o) % 8 * 2 + y_lo}

    def at_member(o):
        return {"member": (m + o) % MEMBERS}

    def at_core():
        return {"tile": xx * 2 + (1 - core)}

    peers = [at_member(o) for o in ORDER] + [at_core()] + [at_x(o) for o in range(1, 4)]

    def load_lat(c):
        rows = pl.ds(pl.multiple_of(c * CROWS, CROWS), CROWS)
        return pltpu.make_async_copy(lat_hbm.at[0, 0, rows, :], lat.at[rows, :], load_sem.at[c])

    load_w = pltpu.make_async_copy(w_in_hbm, w_in, load_sem.at[4])
    load_wo = pltpu.make_async_copy(w_out_hbm, w_raw, load_sem.at[5])
    later = [
        pltpu.make_async_copy(obs_hbm.at[0], obs, load_sem.at[6]),
        pltpu.make_async_copy(idx_hbm, idx, load_sem.at[7]),
        pltpu.make_async_copy(cnt_hbm, cnt, load_sem.at[8]),
    ]
    load_wo.start()
    load_w.start()
    load_lat(0).start()
    x[...] = jnp.zeros(x.shape, F32)
    barrier = pltpu.get_barrier_semaphore()
    for peer in peers:
        pl.semaphore_signal(barrier, inc=1, device_id=peer, device_id_type=MESH)
    for o in (1, 2, 3):
        pl.semaphore_signal(barrier, inc=1, device_id=at_y(o), device_id_type=MESH)
    wo_t[CH:, :] = jnp.zeros((LANE - CH, HID), BF16)
    load_wo.wait()
    wo_t[:CH, :] = w_raw[...]
    wo[...] = wo_t[...].T
    load_w.wait()
    load_lat(0).wait()
    for c in range(1, NCHUNK):
        load_lat(c).start()
    for load in later:
        load.start()

    def there(c, o):
        return pltpu.make_async_remote_copy(
            src_ref=packed.at[c, (m + o) % MEMBERS, pl.ds(0, SENT)], dst_ref=x.at[m, c, pl.ds(0, SENT)],
            send_sem=there_send.at[c, o], recv_sem=there_recv.at[c, o],
            device_id=at_member(o), device_id_type=MESH,
        )

    def returned(c, o):
        return pltpu.make_async_remote_copy(
            src_ref=ret.at[c, (m + o) % MEMBERS, pl.ds(0, SENT)], dst_ref=back.at[c, m, pl.ds(0, SENT)],
            send_sem=back_send.at[c, o], recv_sem=back_recv.at[c, o],
            device_id=at_member(o), device_id_type=MESH,
        )

    def arrived(make, c):
        for o in range(1, MEMBERS):
            make(c, o).wait_recv()

    def forward(c, carry):
        forward_chunk(c, lat, w_in, wo, pre, hid, dec, packed)
        return carry

    def depart(c):
        x[m, c] = packed[c, m]
        for o in ORDER:
            there(c, o).start()

    def forward_and_depart(c, carry):
        load_lat(c).wait()
        forward(c, carry)
        depart(c)
        return carry

    forward(0, 0)
    pl.semaphore_wait(barrier, len(peers) + 3)
    depart(0)
    lax.fori_loop(1, NCHUNK, forward_and_depart, 0)

    for load in later:
        load.wait()
    own_term(obs, idx, cnt, dec, tgt, target, own, weight)
    slopes(pre)
    transposed(hid, hid_t)
    transposed(lat, lat_t)
    sum1[...] = jnp.zeros(sum1.shape, F32)
    sum2[...] = jnp.zeros(sum2.shape, F32)

    def score(c, carry):
        arrived(there, c)
        pair_patch(c, x, part, inv, ret)
        back[c, m] = ret[c, m]
        for o in ORDER:
            returned(c, o).start()
        return carry

    lax.fori_loop(0, NCHUNK, score, 0)

    def backward(c, carry):
        arrived(returned, c)
        grad_chunk(c, back, own, weight, go)
        slope_chunk(c, wo_t, pre, go, gp)
        accumulate(c, hid_t, go, sum2)
        accumulate(c, lat_t, gp, sum1)
        return carry

    lax.fori_loop(0, NCHUNK - 1, backward, 0)
    arrived(returned, NCHUNK - 1)
    grad_chunk(NCHUNK - 1, back, own, weight, go)

    slots = iter(range(SLOTS))
    sent = []

    def send(src, dst, device):
        at = next(slots)
        copy = pltpu.make_async_remote_copy(
            src_ref=src, dst_ref=dst, send_sem=rs_send.at[at], recv_sem=rs_recv.at[at],
            device_id=device, device_id_type=MESH,
        )
        copy.start()
        sent.append(copy)
        return copy

    def added(own_ref, landed, copies):
        for copy in copies:
            copy.wait_recv()
        total = own_ref[...]
        for ref in landed:
            total = total + ref[...]
        own_ref[...] = total

    class Group:
        def __init__(self, q, core_in, hop_in, near_in, far_in, second_in, third_in, at_p, at_q, p, q_at, z_send, z_recv):
            self.q, self.core_in, self.hop_in, self.near_in, self.far_in = q, core_in, hop_in, near_in, far_in
            self.second_in, self.third_in, self.at_p, self.at_q = second_in, third_in, at_p, at_q
            self.p, self.q_at, self.z_send, self.z_recv = p, q_at, z_send, z_recv
            self.core_copy, self.hop, self.near, self.far, self.second = {}, {}, {}, {}, {}

        def part(self, to, h, k):
            return self.q.at[core, to, pl.ds(2 * h, 2), pl.ds(2 * k, 2)]

        def exchange(self, k):
            self.core_copy[k] = send(
                self.q.at[1 - core, :, :, pl.ds(2 * k, 2)], self.core_in.at[k], at_core()
            )

        def first(self, k):
            added(self.q.at[core, :, :, pl.ds(2 * k, 2)], [self.core_in.at[k]], [self.core_copy[k]])
            for h, s in ((0, 1), (1, 3)):
                self.hop[k, h] = send(self.part((self.p + 2) % 4, h, k), self.hop_in.at[k, h], self.at_p(s))
            for h, s in ((0, 1), (1, 3)):
                back_to = 4 - s
                self.near[k, h] = send(
                    self.part((self.p + back_to) % 4, h, k), self.near_in.at[k, h], self.at_p(back_to)
                )

        def relay(self, k):
            for h, s in ((0, 1), (1, 3)):
                added(self.hop_in.at[k, h], [self.part((self.p + s) % 4, h, k)], [self.hop[k, h]])
                self.far[k, h] = send(self.hop_in.at[k, h], self.far_in.at[k, h], self.at_p(s))

        def finish(self, k):
            for h in range(2):
                added(
                    self.part(self.p, h, k), [self.near_in.at[k, h], self.far_in.at[k, h]],
                    [self.near[k, h], self.far[k, h]],
                )

        def other_ring(self, i):
            zs = pl.ds(4 * i, 4)
            self.second[i] = [
                send(self.q.at[core, self.p, (self.q_at + o) % 4, zs], self.second_in.at[i, o - 1], self.at_q(o))
                for o in (2, 1, 3)
            ]

        def collect(self, i):
            landed = [self.second_in.at[i, o] for o in range(3)]
            added(self.q.at[core, self.p, self.q_at, pl.ds(4 * i, 4)], landed, self.second[i])

        def to_z(self, o):
            return pltpu.make_async_remote_copy(
                src_ref=self.q.at[core, self.p, self.q_at, (z + o) % 8], dst_ref=self.third_in.at[o - 1],
                send_sem=self.z_send.at[o - 1], recv_sem=self.z_recv.at[o - 1],
                device_id=at_z(o), device_id_type=MESH,
            )

        def along_z(self, i):
            for j in range(4):
                o = (4 * i + j + 8 - z) % 8

                @pl.when(o != 0)
                def start():
                    self.to_z(o).start()

        def z_copies(self):
            return [self.to_z(o) for o in range(1, 8)]

        def result(self):
            return last(self.q[core, self.p, self.q_at, z], self.third_in, self.z_copies())

    def last(value, landed, copies):
        for copy in copies:
            copy.wait_recv()
        for j in range(landed.shape[0]):
            value = value + landed[j]
        return value

    ga = Group(qa, a0, ah, an, af, a2, a3, at_x, at_y, xx, y, za_send, za_recv)
    gb = Group(qb, b0, bh, bn, bf, b2, b3, at_y, at_x, y, xx, zb_send, zb_recv)
    both = (ga, gb)

    def product(k):
        g = last_chunk(lat_t, gp, sum1, k)
        for j in range(2):
            a_lo, a_hi = halves(g[j, ..., :256], g[j, ..., 256:512])
            b_lo, b_hi = halves(g[j, ..., 512:768], g[j, ..., 768:])
            for lo in range(2):
                for x_ in range(4):
                    for core_ in range(2):
                        qa[core_, x_, lo, 2 * k + j] = a_lo[lo, x_, core_]
                        qa[core_, x_, 2 + lo, 2 * k + j] = a_hi[lo, x_, core_]
                        qb[core_, lo, x_, 2 * k + j] = b_lo[lo, x_, core_]
                        qb[core_, 2 + lo, x_, 2 * k + j] = b_hi[lo, x_, core_]
        for group in both:
            group.exchange(k)

    def each(name, i):
        for group in both:
            getattr(group, name)(i)

    for k in range(4):
        g = last_chunk(hid_t, go, sum2, k)
        for j in range(2):
            c_lo, c_hi = halves(g[j, 0], g[j, 1])
            for x_ in range(4):
                for core_ in range(2):
                    qc[core_, 2 * k + j, x_, 0] = c_lo[x_, core_]
                    qc[core_, 2 * k + j, x_, 1] = c_hi[x_, core_]
    c_core = send(qc.at[1 - core], c0, at_core())
    slope_chunk(NCHUNK - 1, wo_t, pre, go, gp)
    product(0)
    product(1)
    added(qc.at[core], [c0], [c_core])
    c_one = [send(qc.at[core, (z + o) % 8], c1.at[o - 1], at_z(o)) for o in (4, 3, 5, 2, 6, 1, 7)]
    each("first", 0)
    product(2)
    each("first", 1)
    product(3)
    each("relay", 0)
    each("first", 2)
    each("relay", 1)
    each("first", 3)
    each("relay", 2)
    each("relay", 3)
    added(qc.at[core, z], [c1.at[j] for j in range(7)], c_one)
    c_two = [send(qc.at[core, z, (xx + o) % 4], c2.at[o - 1], at_x(o)) for o in (2, 1, 3)]
    each("finish", 0)
    each("finish", 1)
    each("other_ring", 0)
    each("finish", 2)
    each("finish", 3)
    each("other_ring", 1)
    added(qc.at[core, z, xx], [c2.at[j] for j in range(3)], c_two)
    c_three = [send(qc.at[core, z, xx, (y + o) % 4 // 2], c3.at[o - 1], at_y(o)) for o in (2, 1, 3)]
    each("collect", 0)
    each("along_z", 0)
    each("collect", 1)
    each("along_z", 1)
    total = last(qc[core, z, xx, b], c3, c_three)
    out[:, 512:] = jnp.where(y_lo == 0, total, pltpu.roll(total, 4, 0))
    out[:, :256] = ga.result()
    out[:, 256:512] = gb.result()

    for copy in sent + ga.z_copies() + gb.z_copies():
        copy.wait_send()

    def drained(c, carry):
        for o in range(1, MEMBERS):
            there(c, o).wait_send()
            returned(c, o).wait_send()
        return carry

    lax.fori_loop(0, NCHUNK, drained, 0)


def scratch():
    v = pltpu.VMEM
    return [
        v((ROWS, D), BF16), v((D, HID), BF16), v((CH, HID), BF16), v((HID, LANE), BF16), v((LANE, HID), BF16),
        v((POOL, FEAT), BF16), v((1, NPATCH), jnp.int32), v((1, NPATCH), jnp.int32),
        v((ROWS, HID), F32), v((ROWS, HID), BF16), v((NCHUNK, MEMBERS, PATCH, LANE), F32), v((NCHUNK, MEMBERS, PATCH, LANE), F32),
        v((MEMBERS, NCHUNK, PATCH, LANE), F32), v((NPATCH, FEAT), BF16), v((ROWS, LANE), F32),
        v((ROWS, LANE), F32), v((ROWS, LANE), F32), v((len(PAIRS), 8, LANE), F32), v((len(PAIRS), LANE), F32),
        v((NCHUNK, MEMBERS, PATCH, LANE), F32), v((NCHUNK, MEMBERS, PATCH, LANE), F32),
        v((ROWS, LANE), BF16), v((ROWS, HID), BF16), v((D, ROWS), BF16), v((HID, ROWS), BF16),
        v((D, HID), F32), v((HID, LANE), F32),
        v((2, 4, 4, 8, 8, 256), F32), v((2, 4, 4, 8, 8, 256), F32), v((2, 8, 4, 2, 8, 128), F32),
        v((4, 4, 4, 2, 8, 256), F32), v((4, 4, 4, 2, 8, 256), F32), v((8, 4, 2, 8, 128), F32),
        v((4, 2, 2, 2, 8, 256), F32), v((4, 2, 2, 2, 8, 256), F32), v((7, 4, 2, 8, 128), F32),
        v((4, 2, 2, 2, 8, 256), F32), v((4, 2, 2, 2, 8, 256), F32),
        v((4, 2, 2, 2, 8, 256), F32), v((4, 2, 2, 2, 8, 256), F32),
        v((2, 3, 4, 8, 256), F32), v((2, 3, 4, 8, 256), F32), v((3, 2, 8, 128), F32),
        v((7, 8, 256), F32), v((7, 8, 256), F32), v((3, 8, 128), F32),
        pltpu.SemaphoreType.DMA((9,)),
        pltpu.SemaphoreType.DMA((NCHUNK, MEMBERS)), pltpu.SemaphoreType.DMA((NCHUNK, MEMBERS)),
        pltpu.SemaphoreType.DMA((NCHUNK, MEMBERS)), pltpu.SemaphoreType.DMA((NCHUNK, MEMBERS)),
        pltpu.SemaphoreType.DMA((SLOTS,)), pltpu.SemaphoreType.DMA((SLOTS,)),
        pltpu.SemaphoreType.DMA((7,)), pltpu.SemaphoreType.DMA((7,)),
        pltpu.SemaphoreType.DMA((7,)), pltpu.SemaphoreType.DMA((7,)),
    ]


def unpack(packed, out1, out2):
    for i in range(2):
        value = packed[:, i * 256 : i * 256 + 256]
        out1[:, i * 512 : i * 512 + 256] = value[:4]
        out1[:, i * 512 + 256 : i * 512 + 512] = pltpu.roll(value, 4, 0)[:4]
    out2[...] = packed[:4, 512 : 512 + CH]


def shards(latent, w_in, w_out, observed, patch_index, counts):
    packed = pl.pallas_call(
        kernel,
        out_shape=jax.ShapeDtypeStruct((8, 640), F32),
        in_specs=[pl.BlockSpec(memory_space=pl.ANY)] * 6,
        out_specs=pl.BlockSpec(memory_space=pltpu.VMEM),
        scratch_shapes=scratch(),
        compiler_params=pltpu.CompilerParams(
            collective_id=0, has_side_effects=True, vmem_limit_bytes=VMEM_KIB * 1024
        ),
    )(latent, w_in, w_out.T, observed, patch_index, counts)
    return pl.pallas_call(
        unpack,
        out_shape=(jax.ShapeDtypeStruct((4, HID), F32), jax.ShapeDtypeStruct((4, CH), F32)),
        compiler_params=pltpu.CompilerParams(vmem_limit_bytes=1024 * 1024),
    )(packed)


def solution(mesh):
    placed = (
        P("member", "batch", "tile", None),
        P(),
        P(),
        P("batch", "tile", None),
        P("batch", "tile"),
        P("batch", "tile"),
    )
    rows = P(("member", "tile", "batch"), None)
    return jax.shard_map(
        shards, mesh=mesh, in_specs=placed, out_specs=(rows, rows), check_vma=False
    )
```
